32 devices in a mesh: row: 8 (over z, y), col: 4 (over x, core).
Axes of the slice: x: 2, y: 2, z: 4, core: 2. Of those that a mesh axis runs over, the one named last changes fastest.
Arguments:
- feature: bfloat16 [128, 1024, 192], P('row', 'col'), may hold values from -6 to 6
- mask: int32 [128, 1024], P('row', 'col'), may hold values from 0 to 1, as said below
- dw_weight: float32 [7, 7, 192], replicated, may hold values from -1.75 to 1.75
- dw_bias: float32 [192], replicated, may hold values from -3 to 3
- ln_gain: float32 [192], replicated, may hold values from 0.25 to 1.75
- ln_bias: float32 [192], replicated, may hold values from -2.5 to 2.5
- w_in: bfloat16 [192, 768], replicated, may hold values from -0.4375 to 0.4375
- b_in: float32 [768], replicated, may hold values from -3 to 3
- w_out: bfloat16 [768, 192], replicated, may hold values from -0.3125 to 0.3125
- b_out: float32 [192], replicated, may hold values from -2.5 to 2.5
- layer_scale: float32 [192], replicated, may hold values from 0.2 to 1.5
- w_key: bfloat16 [192, 192], replicated, may hold values from -0.4375 to 0.4375
- w_value: bfloat16 [192, 192], replicated, may hold values from -0.4375 to 0.4375
- queries: bfloat16 [512, 192], replicated, may hold values from -160 to 160
- w_proj: bfloat16 [192, 192], replicated, may hold values from -0.4375 to 0.4375
Outputs:
- block_out: bfloat16 [128, 1024, 192], P('row', 'col')
- pooled_out: float32 [512, 192], replicated
The draws below stay inside these ranges and needn't reach their ends.
Inputs may be any that keep to these rules, and one draw needn't show every extreme that they name: `mask`: position (0, 0) is tissue; tissue comes in regions, and some devices' blocks hold none.
All inputs are finite; a program needn't handle non-finite values.
Results may differ from the reference program's by a relative error of at most 0.015.
Values may be sent and summed in bfloat16 or wider, within the bound.
A program may use at most 128 MiB of HBM per device.

```python
import math
import jax
import jax.numpy as jnp
from jax import lax

C = 192
FF = 768
Q = 512
NH = 8
DH = 24
RB = 16
CB = 256
H = 128
W = 1024


def draw_mask(key, part):
    base = jax.random.fold_in(key, 11)
    first, second, third = jax.random.split(base, 3)
    device_level = jax.random.randint(first, (H // RB, W // CB), 0, 5)
    region_draw = jax.random.randint(second, (H // 8, W // 128), 0, 4)
    position_draw = jax.random.randint(third, (H, W), 0, 4)
    level_spread = jnp.repeat(jnp.repeat(device_level, RB // 8, axis=0), CB // 128, axis=1)
    region_on = (region_draw < level_spread).astype(jnp.int32)
    region_full = jnp.repeat(jnp.repeat(region_on, 8, axis=0), 128, axis=1)
    tissue = region_full * (position_draw < 3).astype(jnp.int32)
    return tissue.at[0, 0].set(1).astype(jnp.int32)


def draw_queries(key, part):
    base = jax.random.fold_in(key, 5)
    first = jax.random.fold_in(base, 0)
    values = jnp.clip(jax.random.normal(first, (Q, C), jnp.float32), -4.0, 4.0)
    return values.astype(jnp.bfloat16)


def steps_of(key, shape, cuts, low, high):
    gain, own = 1.0, jax.random.fold_in(key, 6)
    for axis_at, blocks in cuts:
        steps = jnp.exp(jax.random.uniform(jax.random.fold_in(own, axis_at), (blocks,), jnp.float32, low / len(cuts), high / len(cuts)))
        gain = gain * jnp.repeat(steps, shape[axis_at] // blocks).reshape([-1 if axis == axis_at else 1 for axis in range(len(shape))])
    return gain


def centred(key, shape, scale, limit, shards=(), kind=jnp.bfloat16):
    entries = jax.random.normal(key, shape, jnp.float32) * scale
    if len(shards) > 0:
        entries = steps_of(key, shape, shards, -0.22, 0.18) * entries
    return jnp.clip(entries, min=-limit, max=limit).astype(kind)


def setup_inputs(seed: int = 0) -> dict:
    streams_of = jax.random.split(jax.random.key(seed), 16)
    return {
        "feature": centred(streams_of[0], (H, W, C), 1.0, 6.0, ((0, 8), (1, 4))),
        "mask": draw_mask(jax.random.fold_in(streams_of[15], 71), 0),
        "dw_weight": centred(streams_of[2], (7, 7, C), 12 ** -0.5, 1.75, (), jnp.float32),
        "dw_bias": centred(streams_of[3], (C,), 0.5, 3.0, (), jnp.float32),
        "ln_gain": jnp.clip(1.0 + 0.15 * jax.random.normal(streams_of[4], (C,), jnp.float32), 0.25, 1.75),
        "ln_bias": centred(streams_of[5], (C,), 0.4, 2.5, (), jnp.float32),
        "w_in": centred(streams_of[6], (C, FF), C ** -0.5, 0.4375),
        "b_in": centred(streams_of[7], (FF,), 0.5, 3.0, (), jnp.float32),
        "w_out": centred(streams_of[8], (FF, C), (FF // 2) ** -0.5, 0.3125),
        "b_out": centred(streams_of[9], (C,), 0.4, 2.5, (), jnp.float32),
        "layer_scale": jnp.clip(jnp.exp(jax.random.uniform(streams_of[10], (C,), jnp.float32, math.log(0.2), math.log(1.5))), 0.2, 1.5),
        "w_key": centred(streams_of[11], (C, C), C ** -0.5, 0.4375),
        "w_value": centred(streams_of[12], (C, C), C ** -0.5, 0.4375),
        "queries": draw_queries(jax.random.fold_in(streams_of[15], 71), 0),
        "w_proj": centred(streams_of[14], (C, C), C ** -0.5, 0.4375),
    }


def convnext_band(padded_band, center, dw_weight, dw_bias, ln_gain, ln_bias, w_in, b_in, w_out, b_out, layer_scale):
    band_rows = center.shape[0]
    band_cols = center.shape[1]
    conv = jnp.zeros(center.shape, jnp.float32)
    for offset_row in range(7):
        for offset_col in range(7):
            window = padded_band[offset_row:offset_row + band_rows, offset_col:offset_col + band_cols, :]
            conv = conv + window.astype(jnp.float32) * dw_weight[offset_row, offset_col]
    conv = conv + dw_bias
    flat = conv.reshape(-1, conv.shape[-1])
    center_flat = center.reshape(-1, center.shape[-1])
    average = lax.optimization_barrier(jnp.mean(flat, axis=-1, keepdims=True))
    spread = lax.optimization_barrier(jnp.mean((flat - average) ** 2, axis=-1, keepdims=True))
    normed = ((flat - average) * lax.rsqrt(spread + 1e-06) * ln_gain + ln_bias).astype(jnp.bfloat16)
    inner = jnp.dot(normed, w_in, preferred_element_type=jnp.float32) + b_in
    hidden = jax.nn.gelu(inner, approximate=False).astype(jnp.bfloat16)
    branch = jnp.dot(hidden, w_out, preferred_element_type=jnp.float32) + b_out
    result = (center_flat.astype(jnp.float32) + layer_scale * branch).astype(jnp.bfloat16)
    return result.reshape(center.shape)

def pool_group(running, key_group, value_group, mask_group, query_heads, heads, head_size):
    top, total, accum = running
    key_tiles = key_group.reshape(-1, 128, heads, head_size).astype(jnp.float32)
    value_tiles = value_group.reshape(-1, 128, heads, head_size).astype(jnp.float32)
    tissue = mask_group.reshape(-1, 128) > 0
    scores = jnp.einsum('qhd,tphd->thqp', query_heads.astype(jnp.float32), key_tiles) * (1.0 / head_size ** 0.5)
    scores = jnp.where(tissue[:, None, None, :], scores, -jnp.inf)
    tile_top = lax.optimization_barrier(jnp.max(scores, axis=-1))
    safe_top = jnp.where(jnp.isfinite(tile_top), tile_top, 0.0)
    weights = jnp.where(tissue[:, None, None, :], jnp.exp(scores - safe_top[..., None]), 0.0).astype(jnp.bfloat16)
    tile_total = lax.optimization_barrier(jnp.sum(weights.astype(jnp.float32), axis=-1))
    tile_accum = jnp.einsum('thqp,tphd->thqd', weights.astype(jnp.float32), value_tiles)
    new_top = jnp.maximum(top, lax.optimization_barrier(jnp.max(tile_top, axis=0)))
    keep = jnp.exp(top - new_top)
    factor = jnp.exp(tile_top - new_top)
    total = total * keep + lax.optimization_barrier(jnp.sum(factor * tile_total, axis=0))
    accum = accum * keep[..., None] + lax.optimization_barrier(jnp.sum(factor[..., None] * tile_accum, axis=0))
    return (new_top, total, accum)

def reference(feature, mask, dw_weight, dw_bias, ln_gain, ln_bias, w_in, b_in, w_out, b_out, layer_scale, w_key, w_value, queries, w_proj):
    padded = jnp.pad(feature, ((3, 3), (3, 3), (0, 0)))
    band_count = H // RB

    def one_band(index):
        start = (index * RB).astype(jnp.int32)
        padded_band = lax.dynamic_slice_in_dim(padded, start, RB + 6, 0)
        center = lax.dynamic_slice_in_dim(feature, start, RB, 0)
        return convnext_band(padded_band, center, dw_weight, dw_bias, ln_gain, ln_bias, w_in, b_in, w_out, b_out, layer_scale)
    block_out = lax.map(one_band, jnp.arange(band_count, dtype=jnp.int32)).reshape(H, W, C)
    flat = block_out.reshape(-1, C)
    keys = jnp.dot(flat, w_key, preferred_element_type=jnp.float32).astype(jnp.bfloat16)
    values = jnp.dot(flat, w_value, preferred_element_type=jnp.float32).astype(jnp.bfloat16)
    query_heads = queries.reshape(Q, NH, DH)
    group_count = H * W // 512
    inputs = (keys.reshape(group_count, 512, C), values.reshape(group_count, 512, C), mask.reshape(group_count, 512))
    start_state = (jnp.full((NH, Q), -1e+30, jnp.float32), jnp.zeros((NH, Q), jnp.float32), jnp.zeros((NH, Q, DH), jnp.float32))

    def advance(running, items):
        return (pool_group(running, items[0], items[1], items[2], query_heads, NH, DH), None)
    final, unused = lax.scan(advance, start_state, inputs)
    pooled = final[2] / final[1][..., None]
    pooled = jnp.transpose(pooled, (1, 0, 2)).reshape(Q, C).astype(jnp.bfloat16)
    pooled_out = jnp.dot(pooled, w_proj, preferred_element_type=jnp.float32)
    return (block_out, pooled_out)
```

```python
import functools
import math

import jax
import jax.numpy as jnp
from jax import lax
from jax.experimental import pallas as pl
from jax.experimental.pallas import tpu as pltpu
from jax.sharding import PartitionSpec as P

NH = 8
HB = 32
LOW = -1e29
MASKED = -1e30
MESH = pl.DeviceIdType.MESH
SIDES = [(0, -1), (0, 1), (-1, 0), (1, 0), (-1, -1), (-1, 1), (1, -1), (1, 1)]
BF, F32 = jnp.bfloat16, jnp.float32


def lanes(shape, axis=1):
    return lax.broadcasted_iota(jnp.int32, shape, axis)


def front_kernel(
    nr,
    nc,
    x_ref,
    mask_ref,
    dw_ref,
    dwb_ref,
    gain_ref,
    shift_ref,
    win_ref,
    bin_ref,
    wout_ref,
    bout_ref,
    scale_ref,
    wk_ref,
    wv_ref,
    out_ref,
    k_ref,
    vt_ref,
    line_ref,
    strip_ref,
    strip_in,
    corner_ref,
    corner_in,
    s_ref,
    z_ref,
    conv_ref,
    tap_ref,
    base_ref,
    col_ref,
    binc_ref,
    wint_ref,
    wkv_ref,
    send,
    recv,
):
    r, c = lax.axis_index("row"), lax.axis_index("col")
    rows, channels, cols = x_ref.shape
    head = channels // NH

    def inside(dr, dc):
        return (r + dr >= 0) & (r + dr < nr) & (c + dc >= 0) & (c + dc < nc)

    barrier = pltpu.get_barrier_semaphore()
    count = 0
    for dr, dc in SIDES:
        valid = inside(dr, dc)
        count = count + jnp.where(valid, 1, 0)

        @pl.when(valid)
        def _(dr=dr, dc=dc):
            pl.semaphore_signal(barrier, inc=1, device_id=(r + dr, c + dc), device_id_type=MESH)

    lane = lanes((channels, 128))

    def pack(i, carry):
        low, high = carry
        x = x_ref[i].astype(F32)
        own = (lane >= 8 * i) & (lane < 8 * i + 3)
        low = jnp.where(own, pltpu.roll(x[:, 0:128], 8 * i, 1), low)
        high = jnp.where(own, pltpu.roll(x[:, cols - 128 : cols], 8 * i + 3, 1), high)
        return low, high

    zero = jnp.zeros((channels, 128), F32)
    edges = lax.fori_loop(0, rows, pack, (zero, zero))
    for e in range(2):
        strip_ref[e] = edges[e].astype(BF)
        corner_ref[e] = jnp.transpose(edges[e]).astype(BF)

    pl.semaphore_wait(barrier, count)

    def copy(d):
        dr, dc = SIDES[d]
        if dr == 0:
            src = strip_ref.at[0 if dc < 0 else 1]
            dst = strip_in.at[1 if dc < 0 else 0]
        elif dc == 0:
            src = x_ref.at[pl.ds(0 if dr < 0 else rows - 3, 3)]
            dst = line_ref.at[1 if dr < 0 else 0]
        else:
            src = corner_ref.at[0 if dc < 0 else 1, pl.ds(0 if dr < 0 else 96, 32)]
            dst = corner_in.at[pl.ds((64 if dc < 0 else 0) + (32 if dr < 0 else 0), 32)]
        return pltpu.make_async_remote_copy(
            src_ref=src,
            dst_ref=dst,
            send_sem=send.at[d],
            recv_sem=recv.at[d],
            device_id=(r + dr, c + dc),
            device_id_type=MESH,
        )

    for d, (dr, dc) in enumerate(SIDES):

        @pl.when(inside(dr, dc))
        def _(d=d):
            copy(d).start()

        @pl.when(jnp.logical_not(inside(-dr, -dc)))
        def _(d=d, dr=dr, dc=dc):
            if dr == 0:
                strip_in[1 if dc < 0 else 0] = jnp.zeros((channels, 128), BF)
            elif dc == 0:
                line_ref[1 if dr < 0 else 0] = jnp.zeros((3, channels, cols), BF)
            else:
                at = (64 if dc < 0 else 0) + (32 if dr < 0 else 0)
                corner_in[at : at + 32] = jnp.zeros((32, channels), BF)

    tap_ref[...] = jnp.zeros_like(tap_ref)
    for a in range(7):
        for b in range(7):
            at = (b * 16 + a - 3) % 128
            tap_ref[at : at + 1, 0:channels] = dw_ref[a, b : b + 1, :]
    base_ref[...] = jnp.transpose(tap_ref[...])

    def column(vector, size):
        wide = jnp.broadcast_to(vector[None, :], (128, size))
        return jnp.transpose(wide)

    for n, ref in enumerate((dwb_ref, gain_ref, shift_ref, bout_ref, scale_ref)):
        wide = column(ref[...], channels)
        col_ref[n, :, 0:128] = wide
        col_ref[n, :, 128:256] = wide
    wide = column(bin_ref[...], bin_ref.shape[0])
    binc_ref[:, 0:128] = wide
    binc_ref[:, 128:256] = wide
    wint_ref[...] = jnp.transpose(win_ref[...].astype(F32)).astype(BF)
    pad = jnp.zeros((HB - head, channels), F32)
    for n, ref in enumerate((wk_ref, wv_ref)):
        turned = jnp.transpose(ref[...].astype(F32))
        for h in range(NH):
            piece = jnp.concatenate([turned[h * head : (h + 1) * head], pad], axis=0)
            at = n * NH * HB + h * HB
            wkv_ref[at : at + HB, :] = piece.astype(BF)

    def widen(i, carry):
        x = x_ref[i].astype(F32)
        at = pl.multiple_of(i * channels, channels)
        s_ref[0, pl.ds(at, channels)] = x[:, 0:128]
        s_ref[1, pl.ds(at, channels)] = x[:, 128:256]
        return carry

    lax.fori_loop(0, rows, widen, 0)

    def land(d):
        dr, dc = SIDES[d]

        @pl.when(inside(-dr, -dc))
        def _():
            copy(d).wait_recv()

    land(0)
    land(1)

    def side(low, high):
        return jnp.where(lane < 3, low, jnp.where(lane >= 125, high, 0.0))

    def unpack(i, carry):
        left = pltpu.roll(strip_in[0].astype(F32), 125 + (128 - 8 * i), 1)
        right = pltpu.roll(strip_in[1].astype(F32), 128 - 8 * i, 1)
        at = pl.multiple_of(i * channels, channels)
        s_ref[2, pl.ds(at, channels)] = side(right, left)
        return carry

    lax.fori_loop(0, rows, unpack, 0)

    out_row = lanes((rows, 128), 0)
    in_row = lanes((rows, 128), 1) % 16
    near = (in_row - out_row <= 3) & (out_row - in_row <= 3)

    def bands(ch, keep):
        tap = jnp.broadcast_to(base_ref[pl.ds(ch, 1), :], (rows, 128))
        band = jnp.where(keep, pltpu.roll(tap, 0, 1, stride=1, stride_axis=0), 0.0)
        high = band.astype(BF)
        low = (band - high.astype(F32)).astype(BF)
        return jnp.concatenate([high, low], axis=0)

    UN = 8

    def local(step, carry):
        for u in range(UN):
            ch = step * UN + u
            x = jnp.concatenate(
                [s_ref[t, pl.ds(ch, rows, stride=channels), :] for t in range(3)], axis=1
            ).astype(BF)
            parts = [pltpu.roll(x, (3 - b) % 384, 1)[:, 0:cols] for b in range(7)]
            band = bands(ch, near)
            y = jnp.dot(
                band[:, 0:112], jnp.concatenate(parts, axis=0), preferred_element_type=F32
            )
            y = y[0:rows] + y[rows : 2 * rows]
            at = pl.multiple_of(ch * rows, rows)
            conv_ref[0, pl.ds(at, rows)] = y[:, 0:128]
            conv_ref[1, pl.ds(at, rows)] = y[:, 128:256]
        return carry

    lax.fori_loop(0, channels // UN, local, 0)

    hidden_row = lanes((HB * NH, cols), 0)

    def mlp(row):
        flat = jnp.concatenate(
            [conv_ref[t, pl.ds(row, channels, stride=rows), :] for t in range(2)], axis=1
        )
        flat = flat + col_ref[0]
        average = jnp.sum(flat, axis=0, keepdims=True) * (1.0 / channels)
        moved = flat - average
        spread = jnp.sum(moved * moved, axis=0, keepdims=True) * (1.0 / channels)
        normed = (moved * lax.rsqrt(spread + 1e-06) * col_ref[1] + col_ref[2]).astype(BF)
        inner = jnp.dot(wint_ref[...], normed, preferred_element_type=F32) + binc_ref[...]
        act = (0.5 * inner * (1.0 + lax.erf(inner * math.sqrt(0.5)))).astype(BF)
        branch = jnp.dot(wout_ref[...], act, preferred_element_type=F32) + col_ref[3]
        result = (x_ref[row].astype(F32) + col_ref[4] * branch).astype(BF)
        out_ref[row] = result
        both = jnp.dot(wkv_ref[...], result, preferred_element_type=F32)
        bias = jnp.where(mask_ref[pl.ds(row, 1), :] > 0, 0.0, MASKED)
        keys = jnp.where(hidden_row == head, bias, both[0 : NH * HB])
        values = jnp.where(hidden_row % HB == head, 1.0, both[NH * HB : 2 * NH * HB])
        at = pl.multiple_of(row * cols, cols)
        k_ref[pl.ds(at, cols), :] = jnp.transpose(keys).astype(BF)
        vt_ref[:, pl.ds(at, cols)] = values.astype(BF)

    def inner_rows(t, carry):
        mlp(3 + 2 * t)
        mlp(4 + 2 * t)
        return carry

    lax.fori_loop(0, (rows - 6) // 2, inner_rows, 0)

    for d in range(2, 8):
        land(d)

    turned = jnp.transpose(corner_in[...].astype(F32))
    for s in range(8):
        at = s * channels
        if s < 3:
            line = line_ref[1, s].astype(F32)
            right, left = 96 + 8 * s, 32 + 8 * s
        elif s > 4:
            line = line_ref[0, s - 5].astype(F32)
            right, left = 64 + 8 * (s - 4), 8 * (s - 4)
        else:
            for t in range(3):
                z_ref[t, at : at + channels] = zero
            continue
        z_ref[0, at : at + channels] = line[:, 0:128]
        z_ref[1, at : at + channels] = line[:, 128:256]
        z_ref[2, at : at + channels] = side(
            pltpu.roll(turned, 128 - right, 1), pltpu.roll(turned, (125 - left) % 128, 1)
        )

    far = jnp.logical_not(near)

    def outer(step, carry):
        for u in range(UN):
            ch = step * UN + u
            x = jnp.concatenate(
                [z_ref[t, pl.ds(ch, 8, stride=channels), :] for t in range(3)], axis=1
            )
            parts = [pltpu.roll(x, (3 - b) % 384, 1)[:, 0:cols] for b in range(7)]
            groups = []
            for g in range(8):
                groups += [parts[max(g - 1, 0)], parts[(g + 1) % 8 if g != 6 else 0]]
            band = bands(ch, far)
            y = jnp.dot(
                band, jnp.concatenate(groups, axis=0).astype(BF), preferred_element_type=F32
            )
            y = y[0:rows] + y[rows : 2 * rows]
            at = pl.multiple_of(ch * rows, rows)
            conv_ref[0, pl.ds(at, rows)] += y[:, 0:128]
            conv_ref[1, pl.ds(at, rows)] += y[:, 128:256]
        return carry

    lax.fori_loop(0, channels // UN, outer, 0)

    def outer_rows(t, carry):
        mlp(t)
        mlp(rows - 3 + t)
        return carry

    lax.fori_loop(0, 3, outer_rows, 0)

    for d, (dr, dc) in enumerate(SIDES):

        @pl.when(inside(dr, dc))
        def _(d=d):
            copy(d).wait_send()


def front(feature, mask, dw_weight, dw_bias, ln_gain, ln_bias, w_in, b_in, w_out, b_out, scale, wk, wv):
    nr, nc = lax.axis_size("row"), lax.axis_size("col")
    rows, channels, cols = feature.shape
    hidden = w_in.shape[1]
    positions = rows * cols
    wide = NH * HB
    whole = pl.BlockSpec(memory_space=pltpu.VMEM)
    return pl.pallas_call(
        functools.partial(front_kernel, nr, nc),
        out_shape=[
            jax.ShapeDtypeStruct((rows, channels, cols), BF),
            jax.ShapeDtypeStruct((positions, wide), BF),
            jax.ShapeDtypeStruct((wide, positions), BF),
        ],
        in_specs=[whole] * 13,
        out_specs=[whole] * 3,
        scratch_shapes=[
            pltpu.VMEM((2, 3, channels, cols), BF),
            pltpu.VMEM((2, channels, 128), BF),
            pltpu.VMEM((2, channels, 128), BF),
            pltpu.VMEM((2, 128, channels), BF),
            pltpu.VMEM((128, channels), BF),
            pltpu.VMEM((3, rows * channels, 128), F32),
            pltpu.VMEM((3, 8 * channels, 128), F32),
            pltpu.VMEM((2, rows * channels, 128), F32),
            pltpu.VMEM((128, 256), F32),
            pltpu.VMEM((256, 128), F32),
            pltpu.VMEM((5, channels, 256), F32),
            pltpu.VMEM((hidden, 256), F32),
            pltpu.VMEM((hidden, channels), BF),
            pltpu.VMEM((2 * wide, channels), BF),
            pltpu.SemaphoreType.DMA((8,)),
            pltpu.SemaphoreType.DMA((8,)),
        ],
        compiler_params=pltpu.CompilerParams(
            collective_id=1, has_side_effects=True, vmem_limit_bytes=60 << 20
        ),
        name="front",
    )(feature, mask, dw_weight, dw_bias, ln_gain, ln_bias, w_in, b_in, w_out, b_out, scale, wk, wv)


def attend_kernel(k_ref, vt_ref, raw_ref, part_ref, q_ref, sa_ref, sb_ref):
    channels, queries = raw_ref.shape
    head = channels // NH
    positions = k_ref.shape[0]
    qb = sa_ref.shape[1]
    blocks = queries // qb
    total = NH * blocks
    factor = math.log2(math.e) / math.sqrt(head)

    raw = raw_ref[...].astype(F32)
    one = jnp.where(lanes((HB - head, queries), 0) == 0, 1.0, 0.0)
    for h in range(NH):
        q_ref[h] = jnp.zeros((NH * HB, queries), BF)
        if h > 0:
            q_ref[h, 16:32] = jnp.concatenate([jnp.zeros((8, queries), F32), one], axis=0).astype(BF)
        own = jnp.concatenate([raw[h * head : (h + 1) * head], one if h == 0 else one * 0.0], axis=0)
        q_ref[h, h * HB : (h + 1) * HB] = own.astype(BF)

    row = lanes((HB, qb), 0)

    def place(index):
        h = index // blocks
        return h, pl.multiple_of((index - h * blocks) * qb, qb)

    def score(index, s_ref):
        h, at = place(index)
        s = jnp.dot(k_ref[...], q_ref[h, :, pl.ds(at, qb)], preferred_element_type=F32)
        s_ref[...] = s
        return jnp.maximum(jnp.max(s, axis=0, keepdims=True), LOW)

    def absorb(index, s_ref, top):
        h, at = place(index)
        e = jnp.exp2((s_ref[...] - top) * factor).astype(BF)
        v = vt_ref[pl.ds(pl.multiple_of(h * HB, HB), HB), :]
        o = jnp.dot(v, e, preferred_element_type=F32)
        part_ref[h, :, pl.ds(at, qb)] = jnp.where(row == head + 1, top * factor, o)

    top_a = score(0, sa_ref)

    def attend(pair, top_a):
        index = pair * 2
        top_b = score(index + 1, sb_ref)
        absorb(index, sa_ref, top_a)
        top_a = score(jnp.minimum(index + 2, total - 1), sa_ref)
        absorb(index + 1, sb_ref, top_b)
        return top_a

    lax.fori_loop(0, total // 2, attend, top_a)


def attention(keys, values, queries):
    channels, count = queries.shape
    positions, wide = keys.shape
    qb = 256
    whole = pl.BlockSpec(memory_space=pltpu.VMEM)
    return pl.pallas_call(
        attend_kernel,
        out_shape=jax.ShapeDtypeStruct((NH, HB, count), F32),
        in_specs=[whole] * 3,
        out_specs=whole,
        scratch_shapes=[
            pltpu.VMEM((NH, wide, count), BF),
            pltpu.VMEM((positions, qb), F32),
            pltpu.VMEM((positions, qb), F32),
        ],
        compiler_params=pltpu.CompilerParams(vmem_limit_bytes=60 << 20),
        name="attention",
    )(keys, values, queries)


def merge_kernel(
    nr,
    nc,
    part_ref,
    proj_ref,
    out_ref,
    inbox,
    gathered,
    projt_ref,
    send_1,
    recv_1,
    send_2,
    recv_2,
):
    r, c = lax.axis_index("row"), lax.axis_index("col")
    me = r * nc + c
    count = nr * nc
    queries = part_ref.shape[2]
    channels = proj_ref.shape[0]
    head = channels // NH
    tiles = queries // 128
    chunks = NH * tiles
    stride = count // chunks
    mine = lax.rem(me, stride) == 0

    def device(p):
        return (p // nc, lax.rem(p, nc))

    def chunk_of(ref, n):
        h = n // tiles
        at = pl.multiple_of((n - h * tiles) * 128, 128)
        return ref.at[pl.ds(pl.multiple_of(h * HB, HB), HB), pl.ds(at, 128)]

    def part_of(n):
        h = n // tiles
        at = pl.multiple_of((n - h * tiles) * 128, 128)
        return part_ref.at[h, :, pl.ds(at, 128)]

    barrier = pltpu.get_barrier_semaphore()

    def greet(k, carry):
        pl.semaphore_signal(barrier, inc=1, device_id=device(lax.rem(me + k, count)), device_id_type=MESH)
        return carry

    lax.fori_loop(1, count, greet, 0)
    turned = []
    proj = proj_ref[...].astype(F32)
    pad = jnp.zeros((HB - head, channels), F32)
    for h in range(NH):
        turned += [proj[h * head : (h + 1) * head], pad]
    projt_ref[...] = jnp.transpose(jnp.concatenate(turned, axis=0)).astype(BF)
    pl.semaphore_wait(barrier, count - 1)

    def give(k):
        peer = lax.rem(me + k, count)
        return (
            lax.rem(peer, stride) == 0,
            pltpu.make_async_remote_copy(
                src_ref=part_of(peer // stride),
                dst_ref=inbox.at[k - 1],
                send_sem=send_1.at[k - 1],
                recv_sem=recv_1.at[k - 1],
                device_id=device(peer),
                device_id_type=MESH,
            ),
        )

    def give_start(k, carry):
        valid, copy = give(k)

        @pl.when(valid)
        def _():
            copy.start()

        return carry

    lax.fori_loop(1, count, give_start, 0)

    def share(k):
        own = chunk_of(gathered, me // stride)
        return pltpu.make_async_remote_copy(
            src_ref=own,
            dst_ref=own,
            send_sem=send_2.at[k - 1],
            recv_sem=recv_2.at[k - 1],
            device_id=device(lax.rem(me + k, count)),
            device_id_type=MESH,
        )

    row = lanes((HB, 128), 0)

    @pl.when(mine)
    def _():
        def arrive(k, carry):
            give(k)[1].wait_recv()
            return carry

        lax.fori_loop(1, count, arrive, 0)
        own = part_of(me // stride)[...]
        top = own[head + 1 : head + 2]

        def highest(k, top):
            return jnp.maximum(top, inbox[k - 1, head + 1 : head + 2, :])

        top = lax.fori_loop(1, count, highest, top)
        total = own * jnp.exp2(own[head + 1 : head + 2] - top)

        def absorb(k, total):
            piece = inbox[k - 1]
            return total + piece * jnp.exp2(piece[head + 1 : head + 2] - top)

        total = lax.fori_loop(1, count, absorb, total)
        pooled = jnp.where(row < head, total / total[head : head + 1], 0.0)
        chunk_of(gathered, me // stride)[...] = pooled.astype(BF)

        def share_start(k, carry):
            share(k).start()
            return carry

        lax.fori_loop(1, count, share_start, 0)

    def collect(k, carry):
        sender = lax.rem(me - k + count, count)

        @pl.when(lax.rem(sender, stride) == 0)
        def _():
            share(k).wait_recv()

        return carry

    lax.fori_loop(1, count, collect, 0)
    out_ref[...] = jnp.dot(projt_ref[...], gathered[...], preferred_element_type=F32)

    def finish(k, carry):
        valid, copy = give(k)

        @pl.when(valid)
        def _():
            copy.wait_send()

        @pl.when(mine)
        def _():
            share(k).wait_send()

        return carry

    lax.fori_loop(1, count, finish, 0)


def merged(part, proj):
    nr, nc = lax.axis_size("row"), lax.axis_size("col")
    heads, block, queries = part.shape
    channels = proj.shape[0]
    others = nr * nc - 1
    whole = pl.BlockSpec(memory_space=pltpu.VMEM)
    return pl.pallas_call(
        functools.partial(merge_kernel, nr, nc),
        out_shape=jax.ShapeDtypeStruct((channels, queries), F32),
        in_specs=[whole] * 2,
        out_specs=whole,
        scratch_shapes=[
            pltpu.VMEM((others, block, 128), F32),
            pltpu.VMEM((heads * block, queries), BF),
            pltpu.VMEM((channels, heads * block), BF),
        ]
        + [pltpu.SemaphoreType.DMA((others,))] * 4,
        compiler_params=pltpu.CompilerParams(collective_id=0, has_side_effects=True, vmem_limit_bytes=60 << 20),
        name="merge",
    )(part, proj)


def body(
    feature,
    mask,
    dw_weight,
    dw_bias,
    ln_gain,
    ln_bias,
    w_in,
    b_in,
    w_out,
    b_out,
    layer_scale,
    w_key,
    w_value,
    queries,
    w_proj,
):
    block_out, keys, values = front(
        jnp.transpose(feature, (0, 2, 1)),
        mask,
        dw_weight,
        dw_bias,
        ln_gain,
        ln_bias,
        w_in,
        b_in,
        jnp.transpose(w_out),
        b_out,
        layer_scale,
        w_key,
        w_value,
    )
    part = attention(keys, values, jnp.transpose(queries))
    pooled_out = jnp.transpose(merged(part, w_proj))
    return (jnp.transpose(block_out, (0, 2, 1)), pooled_out)


def solution(mesh):
    return jax.shard_map(
        body,
        mesh=mesh,
        in_specs=(P("row", "col", None), P("row", "col")) + (P(),) * 13,
        out_specs=(P("row", "col", None), P()),
        check_vma=False,
    )
```

```python
import functools
import math

import jax
import jax.numpy as jnp
from jax import lax
from jax.experimental import pallas as pl
from jax.experimental.pallas import tpu as pltpu
from jax.sharding import PartitionSpec as P

NH = 8
HB = 32
LOW = -1e29
MASKED = -1e30
MESH = pl.DeviceIdType.MESH
SIDES = [(0, -1), (0, 1), (-1, 0), (1, 0), (-1, -1), (-1, 1), (1, -1), (1, 1)]
BF, F32 = jnp.bfloat16, jnp.float32


def lanes(shape, axis=1):
    return lax.broadcasted_iota(jnp.int32, shape, axis)


def whole_kernel(
    nr,
    nc,
    x_ref,
    mask_ref,
    dw_ref,
    dwb_ref,
    gain_ref,
    shift_ref,
    win_ref,
    bin_ref,
    wout_ref,
    bout_ref,
    scale_ref,
    wk_ref,
    wv_ref,
    raw_ref,
    proj_ref,
    out_ref,
    pooled_ref,
    k_ref,
    vt_ref,
    line_ref,
    strip_ref,
    strip_in,
    corner_ref,
    corner_in,
    s_ref,
    z_ref,
    conv_ref,
    tap_ref,
    base_ref,
    col_ref,
    binc_ref,
    wint_ref,
    wkv_ref,
    q_ref,
    sa_ref,
    sb_ref,
    part_ref,
    inbox,
    gathered,
    projt_ref,
    send,
    recv,
    send_1,
    recv_1,
    send_2,
    recv_2,
):
    r, c = lax.axis_index("row"), lax.axis_index("col")
    rows, channels, cols = x_ref.shape
    head = channels // NH

    def inside(dr, dc):
        return (r + dr >= 0) & (r + dr < nr) & (c + dc >= 0) & (c + dc < nc)

    me = r * nc + c
    count = nr * nc

    def device(p):
        return (p // nc, lax.rem(p, nc))

    barrier = pltpu.get_barrier_semaphore()

    def greet(k, carry):
        pl.semaphore_signal(
            barrier, inc=1, device_id=device(lax.rem(me + k, count)), device_id_type=MESH
        )
        return carry

    lax.fori_loop(1, count, greet, 0)

    lane = lanes((channels, 128))

    def pack(i, carry):
        low, high = carry
        x = x_ref[i].astype(F32)
        own = (lane >= 8 * i) & (lane < 8 * i + 3)
        low = jnp.where(own, pltpu.roll(x[:, 0:128], 8 * i, 1), low)
        high = jnp.where(own, pltpu.roll(x[:, cols - 128 : cols], 8 * i + 3, 1), high)
        return low, high

    zero = jnp.zeros((channels, 128), F32)
    edges = lax.fori_loop(0, rows, pack, (zero, zero))
    for e in range(2):
        strip_ref[e] = edges[e].astype(BF)
        corner_ref[e] = jnp.transpose(edges[e]).astype(BF)

    pl.semaphore_wait(barrier, count - 1)

    def copy(d):
        dr, dc = SIDES[d]
        if dr == 0:
            src = strip_ref.at[0 if dc < 0 else 1]
            dst = strip_in.at[1 if dc < 0 else 0]
        elif dc == 0:
            src = x_ref.at[pl.ds(0 if dr < 0 else rows - 3, 3)]
            dst = line_ref.at[1 if dr < 0 else 0]
        else:
            src = corner_ref.at[0 if dc < 0 else 1, pl.ds(0 if dr < 0 else 96, 32)]
            dst = corner_in.at[pl.ds((64 if dc < 0 else 0) + (32 if dr < 0 else 0), 32)]
        return pltpu.make_async_remote_copy(
            src_ref=src,
            dst_ref=dst,
            send_sem=send.at[d],
            recv_sem=recv.at[d],
            device_id=(r + dr, c + dc),
            device_id_type=MESH,
        )

    for d, (dr, dc) in enumerate(SIDES):

        @pl.when(inside(dr, dc))
        def _(d=d):
            copy(d).start()

        @pl.when(jnp.logical_not(inside(-dr, -dc)))
        def _(d=d, dr=dr, dc=dc):
            if dr == 0:
                strip_in[1 if dc < 0 else 0] = jnp.zeros((channels, 128), BF)
            elif dc == 0:
                line_ref[1 if dr < 0 else 0] = jnp.zeros((3, channels, cols), BF)
            else:
                at = (64 if dc < 0 else 0) + (32 if dr < 0 else 0)
                corner_in[at : at + 32] = jnp.zeros((32, channels), BF)

    tap_ref[...] = jnp.zeros_like(tap_ref)
    for a in range(7):
        for b in range(7):
            at = (b * 16 + a - 3) % 128
            tap_ref[at : at + 1, 0:channels] = dw_ref[a, b : b + 1, :]
    base_ref[...] = jnp.transpose(tap_ref[...])

    def column(vector, size):
        wide = jnp.broadcast_to(vector[None, :], (128, size))
        return jnp.transpose(wide)

    for n, ref in enumerate((dwb_ref, gain_ref, shift_ref, bout_ref, scale_ref)):
        wide = column(ref[...], channels)
        col_ref[n, :, 0:128] = wide
        col_ref[n, :, 128:256] = wide
    wide = column(bin_ref[...], bin_ref.shape[0])
    binc_ref[:, 0:128] = wide
    binc_ref[:, 128:256] = wide
    wint_ref[...] = jnp.transpose(win_ref[...].astype(F32)).astype(BF)
    pad = jnp.zeros((HB - head, channels), F32)
    for n, ref in enumerate((wk_ref, wv_ref)):
        turned = jnp.transpose(ref[...].astype(F32))
        for h in range(NH):
            piece = jnp.concatenate([turned[h * head : (h + 1) * head], pad], axis=0)
            at = n * NH * HB + h * HB
            wkv_ref[at : at + HB, :] = piece.astype(BF)

    turned = []
    proj = proj_ref[...].astype(F32)
    for h in range(NH):
        turned += [proj[h * head : (h + 1) * head], pad]
    projt_ref[...] = jnp.transpose(jnp.concatenate(turned, axis=0)).astype(BF)
    queries = raw_ref.shape[1]
    raw = raw_ref[...].astype(F32)
    one = jnp.where(lanes((HB - head, queries), 0) == 0, 1.0, 0.0)
    for h in range(NH):
        q_ref[h] = jnp.zeros((NH * HB, queries), BF)
        if h > 0:
            q_ref[h, 16:32] = jnp.concatenate([jnp.zeros((8, queries), F32), one], axis=0).astype(BF)
        own = jnp.concatenate([raw[h * head : (h + 1) * head], one if h == 0 else one * 0.0], axis=0)
        q_ref[h, h * HB : (h + 1) * HB] = own.astype(BF)

    def widen(i, carry):
        x = x_ref[i].astype(F32)
        at = pl.multiple_of(i * channels, channels)
        s_ref[0, pl.ds(at, channels)] = x[:, 0:128]
        s_ref[1, pl.ds(at, channels)] = x[:, 128:256]
        return carry

    lax.fori_loop(0, rows, widen, 0)

    def land(d):
        dr, dc = SIDES[d]

        @pl.when(inside(-dr, -dc))
        def _():
            copy(d).wait_recv()

    land(0)
    land(1)

    def side(low, high):
        return jnp.where(lane < 3, low, jnp.where(lane >= 125, high, 0.0))

    def unpack(i, carry):
        left = pltpu.roll(strip_in[0].astype(F32), 125 + (128 - 8 * i), 1)
        right = pltpu.roll(strip_in[1].astype(F32), 128 - 8 * i, 1)
        at = pl.multiple_of(i * channels, channels)
        s_ref[2, pl.ds(at, channels)] = side(right, left)
        return carry

    lax.fori_loop(0, rows, unpack, 0)

    out_row = lanes((rows, 128), 0)
    in_row = lanes((rows, 128), 1) % 16
    near = (in_row - out_row <= 3) & (out_row - in_row <= 3)

    def bands(ch, keep):
        tap = jnp.broadcast_to(base_ref[pl.ds(ch, 1), :], (rows, 128))
        band = jnp.where(keep, pltpu.roll(tap, 0, 1, stride=1, stride_axis=0), 0.0)
        high = band.astype(BF)
        low = (band - high.astype(F32)).astype(BF)
        return jnp.concatenate([high, low], axis=0)

    UN = 8

    def local(step, carry):
        for u in range(UN):
            ch = step * UN + u
            x = jnp.concatenate(
                [s_ref[t, pl.ds(ch, rows, stride=channels), :] for t in range(3)], axis=1
            ).astype(BF)
            parts = [pltpu.roll(x, (3 - b) % 384, 1)[:, 0:cols] for b in range(7)]
            band = bands(ch, near)
            y = jnp.dot(
                band[:, 0:112], jnp.concatenate(parts, axis=0), preferred_element_type=F32
            )
            y = y[0:rows] + y[rows : 2 * rows]
            at = pl.multiple_of(ch * rows, rows)
            conv_ref[0, pl.ds(at, rows)] = y[:, 0:128]
            conv_ref[1, pl.ds(at, rows)] = y[:, 128:256]
        return carry

    lax.fori_loop(0, channels // UN, local, 0)

    hidden_row = lanes((HB * NH, cols), 0)

    def mlp(row):
        flat = jnp.concatenate(
            [conv_ref[t, pl.ds(row, channels, stride=rows), :] for t in range(2)], axis=1
        )
        flat = flat + col_ref[0]
        average = jnp.sum(flat, axis=0, keepdims=True) * (1.0 / channels)
        moved = flat - average
        spread = jnp.sum(moved * moved, axis=0, keepdims=True) * (1.0 / channels)
        normed = (moved * lax.rsqrt(spread + 1e-06) * col_ref[1] + col_ref[2]).astype(BF)
        inner = jnp.dot(wint_ref[...], normed, preferred_element_type=F32) + binc_ref[...]
        act = (0.5 * inner * (1.0 + lax.erf(inner * math.sqrt(0.5)))).astype(BF)
        branch = jnp.dot(wout_ref[...], act, preferred_element_type=F32) + col_ref[3]
        result = (x_ref[row].astype(F32) + col_ref[4] * branch).astype(BF)
        out_ref[row] = result
        both = jnp.dot(wkv_ref[...], result, preferred_element_type=F32)
        bias = jnp.where(mask_ref[pl.ds(row, 1), :] > 0, 0.0, MASKED)
        keys = jnp.where(hidden_row == head, bias, both[0 : NH * HB])
        values = jnp.where(hidden_row % HB == head, 1.0, both[NH * HB : 2 * NH * HB])
        at = pl.multiple_of(row * cols, cols)
        k_ref[pl.ds(at, cols), :] = jnp.transpose(keys).astype(BF)
        vt_ref[:, pl.ds(at, cols)] = values.astype(BF)

    def inner_rows(t, carry):
        mlp(3 + 2 * t)
        mlp(4 + 2 * t)
        return carry

    lax.fori_loop(0, (rows - 6) // 2, inner_rows, 0)

    for d in range(2, 8):
        land(d)

    turned = jnp.transpose(corner_in[...].astype(F32))
    for s in range(8):
        at = s * channels
        if s < 3:
            line = line_ref[1, s].astype(F32)
            right, left = 96 + 8 * s, 32 + 8 * s
        elif s > 4:
            line = line_ref[0, s - 5].astype(F32)
            right, left = 64 + 8 * (s - 4), 8 * (s - 4)
        else:
            for t in range(3):
                z_ref[t, at : at + channels] = zero
            continue
        z_ref[0, at : at + channels] = line[:, 0:128]
        z_ref[1, at : at + channels] = line[:, 128:256]
        z_ref[2, at : at + channels] = side(
            pltpu.roll(turned, 128 - right, 1), pltpu.roll(turned, (125 - left) % 128, 1)
        )

    far = jnp.logical_not(near)

    def outer(step, carry):
        for u in range(UN):
            ch = step * UN + u
            x = jnp.concatenate(
                [z_ref[t, pl.ds(ch, 8, stride=channels), :] for t in range(3)], axis=1
            )
            parts = [pltpu.roll(x, (3 - b) % 384, 1)[:, 0:cols] for b in range(7)]
            groups = []
            for g in range(8):
                groups += [parts[max(g - 1, 0)], parts[(g + 1) % 8 if g != 6 else 0]]
            band = bands(ch, far)
            y = jnp.dot(
                band, jnp.concatenate(groups, axis=0).astype(BF), preferred_element_type=F32
            )
            y = y[0:rows] + y[rows : 2 * rows]
            at = pl.multiple_of(ch * rows, rows)
            conv_ref[0, pl.ds(at, rows)] += y[:, 0:128]
            conv_ref[1, pl.ds(at, rows)] += y[:, 128:256]
        return carry

    lax.fori_loop(0, channels // UN, outer, 0)

    def outer_rows(t, carry):
        mlp(t)
        mlp(rows - 3 + t)
        return carry

    lax.fori_loop(0, 3, outer_rows, 0)

    qb = sa_ref.shape[1]
    blocks = queries // qb
    total = NH * blocks
    factor = math.log2(math.e) / math.sqrt(head)
    per = qb // 128
    chunks = total * per
    stride = count // chunks
    row = lanes((HB, qb), 0)

    def owner(n):
        return lax.rem(n * 11 + 31, chunks) * stride

    mine = lax.rem(me, stride) == 0
    own_chunk = lax.rem((me // stride + 1) * 3, chunks)

    def place(index):
        h = index // blocks
        return h, pl.multiple_of((index - h * blocks) * qb, qb)

    def score(index, s_ref):
        h, at = place(index)
        s = jnp.dot(k_ref[...], q_ref[h, :, pl.ds(at, qb)], preferred_element_type=F32)
        s_ref[...] = s
        return jnp.maximum(jnp.max(s, axis=0, keepdims=True), LOW)

    def absorb(index, s_ref, top):
        h, at = place(index)
        e = jnp.exp2((s_ref[...] - top) * factor).astype(BF)
        v = vt_ref[pl.ds(pl.multiple_of(h * HB, HB), HB), :]
        o = jnp.dot(v, e, preferred_element_type=F32)
        o = jnp.where(row == head + 1, top * factor, o)
        for n in range(per):
            part_ref[index * per + n] = o[:, n * 128 : n * 128 + 128]

    def give(n, k):
        return pltpu.make_async_remote_copy(
            src_ref=part_ref.at[n],
            dst_ref=inbox.at[k - 1],
            send_sem=send_1.at[n],
            recv_sem=recv_1.at[k - 1],
            device_id=device(owner(n)),
            device_id_type=MESH,
        )

    def away(n):
        return lax.rem(owner(n) - me + count, count)

    def chunk_of(n):
        h = n // (blocks * per)
        at = pl.multiple_of((n - h * blocks * per) * 128, 128)
        return gathered.at[pl.ds(pl.multiple_of(h * HB, HB), HB), pl.ds(at, 128)]

    def share(k, n):
        return pltpu.make_async_remote_copy(
            src_ref=chunk_of(n),
            dst_ref=chunk_of(n),
            send_sem=send_2.at[k - 1],
            recv_sem=recv_2.at[n],
            device_id=device(lax.rem(me + k, count)),
            device_id_type=MESH,
        )

    def hand_out(pair):
        for n in range(2 * per):
            chunk = pair * 2 * per + n

            @pl.when(owner(chunk) != me)
            def _(chunk=chunk):
                give(chunk, away(chunk)).start()

    row1 = lanes((HB, 128), 0)

    def finish():
        def arrive(k, carry):
            give(own_chunk, k).wait_recv()
            return carry

        lax.fori_loop(1, count, arrive, 0)
        piece = part_ref[own_chunk]
        level = piece[head + 1 : head + 2]

        def highest(k, top):
            return jnp.maximum(top, inbox[k - 1, head + 1 : head + 2, :])

        top = lax.fori_loop(1, count, highest, level)

        def add(k, total):
            piece = inbox[k - 1]
            return total + piece * jnp.exp2(piece[head + 1 : head + 2] - top)

        summed = lax.fori_loop(1, count, add, piece * jnp.exp2(level - top))
        pooled = jnp.where(row1 < head, summed / summed[head : head + 1], 0.0)
        chunk_of(own_chunk)[...] = pooled.astype(BF)

        def share_start(k, carry):
            share(k, own_chunk).start()
            return carry

        lax.fori_loop(1, count, share_start, 0)

    LAG = 2
    own_pair = own_chunk // (2 * per)
    top_a = score(0, sa_ref)

    def attend(pair, top_a):
        index = pair * 2
        top_b = score(index + 1, sb_ref)
        absorb(index, sa_ref, top_a)
        top_a = score(index + 2, sa_ref)
        absorb(index + 1, sb_ref, top_b)
        hand_out(pair)

        @pl.when(mine & (own_pair + LAG == pair))
        def _():
            finish()

        return top_a

    pairs = total // 2
    top_a = lax.fori_loop(0, pairs - 1, attend, top_a)
    top_b = score(total - 1, sb_ref)
    absorb(total - 2, sa_ref, top_a)
    absorb(total - 1, sb_ref, top_b)
    hand_out(pairs - 1)

    @pl.when(mine & (own_pair + LAG >= pairs - 1))
    def _():
        finish()

    def collect(n, carry):
        @pl.when(owner(n) != me)
        def _():
            share(1, n).wait_recv()

        return carry

    lax.fori_loop(0, chunks, collect, 0)
    pooled_ref[...] = jnp.dot(projt_ref[...], gathered[...], preferred_element_type=F32)

    def given(n, carry):
        @pl.when(owner(n) != me)
        def _():
            give(n, away(n)).wait_send()

        return carry

    lax.fori_loop(0, chunks, given, 0)

    @pl.when(mine)
    def _():
        def shared(k, carry):
            share(k, own_chunk).wait_send()
            return carry

        lax.fori_loop(1, count, shared, 0)

    for d, (dr, dc) in enumerate(SIDES):

        @pl.when(inside(dr, dc))
        def _(d=d):
            copy(d).wait_send()


def whole(feature, mask, dw_weight, dw_bias, ln_gain, ln_bias, w_in, b_in, w_out, b_out, scale, wk, wv, queries, proj):
    nr, nc = lax.axis_size("row"), lax.axis_size("col")
    rows, channels, cols = feature.shape
    hidden = w_in.shape[1]
    positions = rows * cols
    wide = NH * HB
    number = queries.shape[1]
    qb = 256
    chunks = NH * number // 128
    others = nr * nc - 1
    full = pl.BlockSpec(memory_space=pltpu.VMEM)
    return pl.pallas_call(
        functools.partial(whole_kernel, nr, nc),
        out_shape=[
            jax.ShapeDtypeStruct((rows, channels, cols), BF),
            jax.ShapeDtypeStruct((channels, number), F32),
        ],
        in_specs=[full] * 15,
        out_specs=[full] * 2,
        scratch_shapes=[
            pltpu.VMEM((positions, wide), BF),
            pltpu.VMEM((wide, positions), BF),
            pltpu.VMEM((2, 3, channels, cols), BF),
            pltpu.VMEM((2, channels, 128), BF),
            pltpu.VMEM((2, channels, 128), BF),
            pltpu.VMEM((2, 128, channels), BF),
            pltpu.VMEM((128, channels), BF),
            pltpu.VMEM((3, rows * channels, 128), F32),
            pltpu.VMEM((3, 8 * channels, 128), F32),
            pltpu.VMEM((2, rows * channels, 128), F32),
            pltpu.VMEM((128, 256), F32),
            pltpu.VMEM((256, 128), F32),
            pltpu.VMEM((5, channels, 256), F32),
            pltpu.VMEM((hidden, 256), F32),
            pltpu.VMEM((hidden, channels), BF),
            pltpu.VMEM((2 * wide, channels), BF),
            pltpu.VMEM((NH, wide, number), BF),
            pltpu.VMEM((positions, qb), F32),
            pltpu.VMEM((positions, qb), F32),
            pltpu.VMEM((chunks, HB, 128), F32),
            pltpu.VMEM((others, HB, 128), F32),
            pltpu.VMEM((wide, number), BF),
            pltpu.VMEM((channels, wide), BF),
            pltpu.SemaphoreType.DMA((8,)),
            pltpu.SemaphoreType.DMA((8,)),
            pltpu.SemaphoreType.DMA((chunks,)),
            pltpu.SemaphoreType.DMA((others,)),
            pltpu.SemaphoreType.DMA((others,)),
            pltpu.SemaphoreType.DMA((chunks,)),
        ],
        compiler_params=pltpu.CompilerParams(
            collective_id=0, has_side_effects=True, vmem_limit_bytes=60 << 20
        ),
        name="whole",
    )(feature, mask, dw_weight, dw_bias, ln_gain, ln_bias, w_in, b_in, w_out, b_out, scale, wk, wv, queries, proj)


def body(
    feature,
    mask,
    dw_weight,
    dw_bias,
    ln_gain,
    ln_bias,
    w_in,
    b_in,
    w_out,
    b_out,
    layer_scale,
    w_key,
    w_value,
    queries,
    w_proj,
):
    block_out, pooled = whole(
        jnp.transpose(feature, (0, 2, 1)),
        mask,
        dw_weight,
        dw_bias,
        ln_gain,
        ln_bias,
        w_in,
        b_in,
        jnp.transpose(w_out),
        b_out,
        layer_scale,
        w_key,
        w_value,
        jnp.transpose(queries),
        w_proj,
    )
    return (jnp.transpose(block_out, (0, 2, 1)), jnp.transpose(pooled))


def solution(mesh):
    return jax.shard_map(
        body,
        mesh=mesh,
        in_specs=(P("row", "col", None), P("row", "col")) + (P(),) * 13,
        out_specs=(P("row", "col", None), P()),
        check_vma=False,
    )
```

```python
import functools
import math

import jax
import jax.numpy as jnp
from jax import lax
from jax.experimental import pallas as pl
from jax.experimental.pallas import tpu as pltpu
from jax.sharding import PartitionSpec as P

NH = 8
HB = 32
LOW = -1e29
MASKED = -1e30
MESH = pl.DeviceIdType.MESH
SIDES = [(0, -1), (0, 1), (-1, 0), (1, 0), (-1, -1), (-1, 1), (1, -1), (1, 1)]
BF, F32 = jnp.bfloat16, jnp.float32


def lanes(shape, axis=1):
    return lax.broadcasted_iota(jnp.int32, shape, axis)


def whole_kernel(
    nr,
    nc,
    x_ref,
    mask_ref,
    dw_ref,
    dwb_ref,
    gain_ref,
    shift_ref,
    win_ref,
    bin_ref,
    wout_ref,
    bout_ref,
    scale_ref,
    wk_ref,
    wv_ref,
    raw_ref,
    proj_ref,
    out_ref,
    pooled_ref,
    k_ref,
    vt_ref,
    line_ref,
    strip_ref,
    strip_in,
    corner_ref,
    corner_in,
    s_ref,
    z_ref,
    conv_ref,
    tap_ref,
    base_ref,
    col_ref,
    half_ref,
    wint_ref,
    wkv_ref,
    q_ref,
    sa_ref,
    sb_ref,
    part_ref,
    pair_ref,
    inbox,
    gathered,
    projt_ref,
    send,
    recv,
    send_0,
    recv_0,
    send_1,
    recv_1,
    send_2,
    recv_2,
):
    r, c = lax.axis_index("row"), lax.axis_index("col")
    rows, channels, cols = x_ref.shape
    head = channels // NH

    def inside(dr, dc):
        return (r + dr >= 0) & (r + dr < nr) & (c + dc >= 0) & (c + dc < nc)

    me = r * nc + c
    count = nr * nc

    def device(p):
        return (p // nc, lax.rem(p, nc))

    barrier = pltpu.get_barrier_semaphore()

    def greet(k, carry):
        pl.semaphore_signal(
            barrier, inc=1, device_id=device(lax.rem(me + k, count)), device_id_type=MESH
        )
        return carry

    lax.fori_loop(1, count, greet, 0)

    lane = lanes((channels, 128))

    def pack(i, carry):
        low, high = carry
        x = x_ref[i].astype(F32)
        own = (lane >= 8 * i) & (lane < 8 * i + 3)
        low = jnp.where(own, pltpu.roll(x[:, 0:128], 8 * i, 1), low)
        high = jnp.where(own, pltpu.roll(x[:, cols - 128 : cols], 8 * i + 3, 1), high)
        return low, high

    zero = jnp.zeros((channels, 128), F32)
    edges = lax.fori_loop(0, rows, pack, (zero, zero))
    for e in range(2):
        strip_ref[e] = edges[e].astype(BF)
        corner_ref[e] = jnp.transpose(edges[e]).astype(BF)

    pl.semaphore_wait(barrier, count - 1)

    def copy(d):
        dr, dc = SIDES[d]
        if dr == 0:
            src = strip_ref.at[0 if dc < 0 else 1]
            dst = strip_in.at[1 if dc < 0 else 0]
        elif dc == 0:
            src = x_ref.at[pl.ds(0 if dr < 0 else rows - 3, 3)]
            dst = line_ref.at[1 if dr < 0 else 0]
        else:
            src = corner_ref.at[0 if dc < 0 else 1, pl.ds(0 if dr < 0 else 96, 32)]
            dst = corner_in.at[pl.ds((64 if dc < 0 else 0) + (32 if dr < 0 else 0), 32)]
        return pltpu.make_async_remote_copy(
            src_ref=src,
            dst_ref=dst,
            send_sem=send.at[d],
            recv_sem=recv.at[d],
            device_id=(r + dr, c + dc),
            device_id_type=MESH,
        )

    for d, (dr, dc) in enumerate(SIDES):

        @pl.when(inside(dr, dc))
        def _(d=d):
            copy(d).start()

        @pl.when(jnp.logical_not(inside(-dr, -dc)))
        def _(d=d, dr=dr, dc=dc):
            if dr == 0:
                strip_in[1 if dc < 0 else 0] = jnp.zeros((channels, 128), BF)
            elif dc == 0:
                line_ref[1 if dr < 0 else 0] = jnp.zeros((3, channels, cols), BF)
            else:
                at = (64 if dc < 0 else 0) + (32 if dr < 0 else 0)
                corner_in[at : at + 32] = jnp.zeros((32, channels), BF)

    tap_ref[...] = jnp.zeros_like(tap_ref)
    for a in range(7):
        for b in range(7):
            at = (b * 16 + a - 3) % 128
            tap_ref[at : at + 1, 0:channels] = dw_ref[a, b : b + 1, :]
    base_ref[...] = jnp.transpose(tap_ref[...])

    def column(vector, size):
        wide = jnp.broadcast_to(vector[None, :], (128, size))
        return jnp.transpose(wide)

    for n, ref in enumerate((dwb_ref, gain_ref, shift_ref, bout_ref, scale_ref)):
        wide = column(ref[...], channels)
        col_ref[n, :, 0:128] = wide
        col_ref[n, :, 128:256] = wide
    level = jnp.broadcast_to(bin_ref[...][None, :], (8, bin_ref.shape[0]))
    row8 = lanes(level.shape, 0)
    terms = jnp.zeros_like(level)
    for n in range(3):
        term = level.astype(BF).astype(F32)
        terms = jnp.where(row8 == n, term, terms)
        level = level - term
    stack = jnp.concatenate([win_ref[...].astype(F32), terms, jnp.zeros_like(terms)], axis=0)
    wint_ref[...] = jnp.transpose(stack).astype(BF)
    half_ref[...] = (wout_ref[...].astype(F32) * 0.5).astype(BF)
    pad = jnp.zeros((HB - head, channels), F32)
    mark_row, mark_lane = lanes((HB, 16), 0), lanes((HB, 16), 1)
    for n, ref in enumerate((wk_ref, wv_ref)):
        turned = jnp.transpose(ref[...].astype(F32))
        for h in range(NH):
            piece = jnp.concatenate([turned[h * head : (h + 1) * head], pad], axis=0)
            tag = 1.0 if n == 1 else (1.0 if h == 0 else 0.0)
            mark = jnp.where((mark_row == head) & (mark_lane == (0 if n == 1 else 1)), tag, 0.0)
            at = n * NH * HB + h * HB
            wkv_ref[at : at + HB, :] = jnp.concatenate([piece, mark], axis=1).astype(BF)

    turned = []
    proj = proj_ref[...].astype(F32)
    for h in range(NH):
        turned += [proj[h * head : (h + 1) * head], pad]
    projt_ref[...] = jnp.transpose(jnp.concatenate(turned, axis=0)).astype(BF)
    queries = raw_ref.shape[1]
    raw = raw_ref[...].astype(F32)
    one = jnp.where(lanes((HB - head, queries), 0) == 0, 1.0, 0.0)
    for h in range(NH):
        q_ref[h] = jnp.zeros((NH * HB, queries), BF)
        if h > 0:
            q_ref[h, 16:32] = jnp.concatenate([jnp.zeros((8, queries), F32), one], axis=0).astype(BF)
        own = jnp.concatenate([raw[h * head : (h + 1) * head], one if h == 0 else one * 0.0], axis=0)
        q_ref[h, h * HB : (h + 1) * HB] = own.astype(BF)

    def widen(i, carry):
        x = x_ref[i].astype(F32)
        at = pl.multiple_of(i * channels, channels)
        s_ref[0, pl.ds(at, channels)] = x[:, 0:128]
        s_ref[1, pl.ds(at, channels)] = x[:, 128:256]
        return carry

    lax.fori_loop(0, rows, widen, 0)

    def land(d):
        dr, dc = SIDES[d]

        @pl.when(inside(-dr, -dc))
        def _():
            copy(d).wait_recv()

    land(0)
    land(1)

    def side(low, high):
        return jnp.where(lane < 3, low, jnp.where(lane >= 125, high, 0.0))

    def unpack(i, carry):
        left = pltpu.roll(strip_in[0].astype(F32), 125 + (128 - 8 * i), 1)
        right = pltpu.roll(strip_in[1].astype(F32), 128 - 8 * i, 1)
        at = pl.multiple_of(i * channels, channels)
        s_ref[2, pl.ds(at, channels)] = side(right, left)
        return carry

    lax.fori_loop(0, rows, unpack, 0)

    out_row = lanes((rows, 128), 0)
    in_row = lanes((rows, 128), 1) % 16
    near = (in_row - out_row <= 3) & (out_row - in_row <= 3)

    def bands(ch, keep):
        tap = jnp.broadcast_to(base_ref[pl.ds(ch, 1), :], (rows, 128))
        band = jnp.where(keep, pltpu.roll(tap, 0, 1, stride=1, stride_axis=0), 0.0)
        high = band.astype(BF)
        low = (band - high.astype(F32)).astype(BF)
        return jnp.concatenate([high, low], axis=0)

    UN = 32

    def local(step, carry):
        for u in range(UN):
            ch = step * UN + u
            x = jnp.concatenate(
                [s_ref[t, pl.ds(ch, rows, stride=channels), :] for t in range(3)], axis=1
            ).astype(BF)
            parts = [pltpu.roll(x, (3 - b) % 384, 1)[:, 0:cols] for b in range(7)]
            band = bands(ch, near)
            y = jnp.dot(
                band[:, 0:112], jnp.concatenate(parts, axis=0), preferred_element_type=F32
            )
            y = y[0:rows] + y[rows : 2 * rows]
            at = pl.multiple_of(ch * rows, rows)
            conv_ref[0, pl.ds(at, rows)] = y[:, 0:128]
            conv_ref[1, pl.ds(at, rows)] = y[:, 128:256]
        return carry

    lax.fori_loop(0, channels // UN, local, 0)

    row16 = lanes((16, cols), 0)
    ones16 = jnp.where(row16 < 3, 1.0, 0.0).astype(BF)

    def mlp(row):
        flat = jnp.concatenate(
            [conv_ref[t, pl.ds(row, channels, stride=rows), :] for t in range(2)], axis=1
        )
        flat = flat + col_ref[0]
        average = jnp.sum(flat, axis=0, keepdims=True) * (1.0 / channels)
        moved = flat - average
        spread = jnp.sum(moved * moved, axis=0, keepdims=True) * (1.0 / channels)
        normed = (moved * lax.rsqrt(spread + 1e-06) * col_ref[1] + col_ref[2]).astype(BF)
        normed = jnp.concatenate([normed, ones16], axis=0)
        inner = jnp.dot(wint_ref[...], normed, preferred_element_type=F32)
        act = (inner * (1.0 + lax.erf(inner * math.sqrt(0.5)))).astype(BF)
        branch = jnp.dot(half_ref[...], act, preferred_element_type=F32) + col_ref[3]
        result = (x_ref[row].astype(F32) + col_ref[4] * branch).astype(BF)
        out_ref[row] = result
        bias = jnp.where(mask_ref[pl.ds(row, 1), :] > 0, 0.0, MASKED)
        extra = jnp.where(row16 == 0, 1.0, jnp.where(row16 == 1, bias, 0.0)).astype(BF)
        result = jnp.concatenate([result, extra], axis=0)
        both = jnp.dot(wkv_ref[...], result, preferred_element_type=F32)
        keys, values = both[0 : NH * HB], both[NH * HB : 2 * NH * HB]
        at = pl.multiple_of(row * cols, cols)
        k_ref[pl.ds(at, cols), :] = jnp.transpose(keys).astype(BF)
        vt_ref[:, pl.ds(at, cols)] = values.astype(BF)

    def inner_rows(t, carry):
        for n in range(5):
            mlp(3 + 5 * t + n)
        return carry

    lax.fori_loop(0, (rows - 6) // 5, inner_rows, 0)

    for d in range(2, 8):
        land(d)

    turned = jnp.transpose(corner_in[...].astype(F32))
    for s in range(8):
        at = s * channels
        if s < 3:
            line = line_ref[1, s].astype(F32)
            right, left = 96 + 8 * s, 32 + 8 * s
        elif s > 4:
            line = line_ref[0, s - 5].astype(F32)
            right, left = 64 + 8 * (s - 4), 8 * (s - 4)
        else:
            for t in range(3):
                z_ref[t, at : at + channels] = zero
            continue
        z_ref[0, at : at + channels] = line[:, 0:128]
        z_ref[1, at : at + channels] = line[:, 128:256]
        z_ref[2, at : at + channels] = side(
            pltpu.roll(turned, 128 - right, 1), pltpu.roll(turned, (125 - left) % 128, 1)
        )

    far = jnp.logical_not(near)

    def outer(step, carry):
        for u in range(UN):
            ch = step * UN + u
            x = jnp.concatenate(
                [z_ref[t, pl.ds(ch, 8, stride=channels), :] for t in range(3)], axis=1
            )
            parts = [pltpu.roll(x, (3 - b) % 384, 1)[:, 0:cols] for b in range(7)]
            groups = []
            for g in range(8):
                groups += [parts[max(g - 1, 0)], parts[(g + 1) % 8 if g != 6 else 0]]
            band = bands(ch, far)
            y = jnp.dot(
                band, jnp.concatenate(groups, axis=0).astype(BF), preferred_element_type=F32
            )
            y = y[0:rows] + y[rows : 2 * rows]
            at = pl.multiple_of(ch * rows, rows)
            conv_ref[0, pl.ds(at, rows)] += y[:, 0:128]
            conv_ref[1, pl.ds(at, rows)] += y[:, 128:256]
        return carry

    lax.fori_loop(0, channels // UN, outer, 0)

    def outer_rows(t, carry):
        for n in range(3):
            mlp((rows - 3) * t + n)
        return carry

    lax.fori_loop(0, 2, outer_rows, 0)

    qb = sa_ref.shape[1]
    blocks = queries // qb
    total = NH * blocks
    factor = math.log2(math.e) / math.sqrt(head)
    per = qb // 128
    chunks = total * per
    stride = count // chunks
    row = lanes((HB, qb), 0)

    def owner(n):
        return lax.rem(n * 11 + 31, chunks) * stride

    mine = lax.rem(me, stride) == 0
    own_chunk = lax.rem((me // stride + 1) * 3, chunks)

    def place(index):
        h = index // blocks
        return h, pl.multiple_of((index - h * blocks) * qb, qb)

    def score(index, s_ref):
        h, at = place(index)
        s = jnp.dot(k_ref[...], q_ref[h, :, pl.ds(at, qb)], preferred_element_type=F32)
        s_ref[...] = s
        return jnp.maximum(jnp.max(s, axis=0, keepdims=True), LOW)

    def absorb(index, s_ref, top):
        h, at = place(index)
        e = jnp.exp2((s_ref[...] - top) * factor).astype(BF)
        v = vt_ref[pl.ds(pl.multiple_of(h * HB, HB), HB), :]
        o = jnp.dot(v, e, preferred_element_type=F32)
        o = jnp.where(row == head + 1, top * factor, o)
        for n in range(per):
            part_ref[index * per + n] = o[:, n * 128 : n * 128 + 128]

    chip, core = me // 2, lax.rem(me, 2)
    chips = count // 2

    def pass_on(n):
        return pltpu.make_async_remote_copy(
            src_ref=part_ref.at[n],
            dst_ref=pair_ref.at[n],
            send_sem=send_0.at[n],
            recv_sem=recv_0.at[n],
            device_id=device(chip * 2 + 1 - core),
            device_id_type=MESH,
        )

    def give(n, k):
        return pltpu.make_async_remote_copy(
            src_ref=part_ref.at[n],
            dst_ref=inbox.at[k - 1],
            send_sem=send_1.at[n],
            recv_sem=recv_1.at[k - 1],
            device_id=device(owner(n)),
            device_id_type=MESH,
        )

    def away(n):
        return lax.rem(owner(n) // 2 - chip + chips, chips)

    def same_core(n):
        return lax.rem(owner(n), 2) == core

    def chunk_of(n):
        h = n // (blocks * per)
        at = pl.multiple_of((n - h * blocks * per) * 128, 128)
        return gathered.at[pl.ds(pl.multiple_of(h * HB, HB), HB), pl.ds(at, 128)]

    def share(k, n):
        return pltpu.make_async_remote_copy(
            src_ref=chunk_of(n),
            dst_ref=chunk_of(n),
            send_sem=send_2.at[k - 1],
            recv_sem=recv_2.at[n],
            device_id=device(lax.rem(me + k, count)),
            device_id_type=MESH,
        )

    row1 = lanes((HB, 128), 0)

    def hand_over(pair):
        for n in range(2 * per):
            chunk = pair * 2 * per + n

            @pl.when(jnp.logical_not(same_core(chunk)))
            def _(chunk=chunk):
                pass_on(chunk).start()

    def hand_out(pair):
        for n in range(2 * per):
            chunk = pair * 2 * per + n

            @pl.when(same_core(chunk))
            def _(chunk=chunk):
                pass_on(chunk).wait_recv()
                one, two = part_ref[chunk], pair_ref[chunk]
                first, second = one[head + 1 : head + 2], two[head + 1 : head + 2]
                top = jnp.maximum(first, second)
                both = one * jnp.exp2(first - top) + two * jnp.exp2(second - top)
                part_ref[chunk] = jnp.where(row1 == head + 1, top, both)

                @pl.when(owner(chunk) != me)
                def _():
                    give(chunk, away(chunk)).start()

    def finish():
        def arrive(k, carry):
            give(own_chunk, k).wait_recv()
            return carry

        lax.fori_loop(1, chips, arrive, 0)
        piece = part_ref[own_chunk]
        level = piece[head + 1 : head + 2]

        def highest(k, top):
            return jnp.maximum(top, inbox[k - 1, head + 1 : head + 2, :])

        top = lax.fori_loop(1, chips, highest, level)

        def add(k, total):
            piece = inbox[k - 1]
            return total + piece * jnp.exp2(piece[head + 1 : head + 2] - top)

        summed = lax.fori_loop(1, chips, add, piece * jnp.exp2(level - top))
        pooled = jnp.where(row1 < head, summed / summed[head : head + 1], 0.0)
        chunk_of(own_chunk)[...] = pooled.astype(BF)

        def share_start(k, carry):
            share(k, own_chunk).start()
            return carry

        lax.fori_loop(1, count, share_start, 0)

    LAG = 3
    own_pair = own_chunk // (2 * per)
    top_a = score(0, sa_ref)

    def attend(pair, top_a):
        index = pair * 2
        top_b = score(index + 1, sb_ref)
        absorb(index, sa_ref, top_a)
        top_a = score(index + 2, sa_ref)
        absorb(index + 1, sb_ref, top_b)
        hand_over(pair)

        @pl.when(pair > 0)
        def _():
            hand_out(pair - 1)

        @pl.when(mine & (own_pair + LAG == pair))
        def _():
            finish()

        return top_a

    pairs = total // 2
    top_a = lax.fori_loop(0, pairs - 1, attend, top_a)
    top_b = score(total - 1, sb_ref)
    absorb(total - 2, sa_ref, top_a)
    absorb(total - 1, sb_ref, top_b)
    hand_over(pairs - 1)
    hand_out(pairs - 2)
    hand_out(pairs - 1)

    @pl.when(mine & (own_pair + LAG >= pairs - 1))
    def _():
        finish()

    def collect(n, carry):
        @pl.when(owner(n) != me)
        def _():
            share(1, n).wait_recv()

        return carry

    lax.fori_loop(0, chunks, collect, 0)
    pooled_ref[...] = jnp.dot(projt_ref[...], gathered[...], preferred_element_type=F32)

    def given(n, carry):
        @pl.when(same_core(n) & (owner(n) != me))
        def _():
            give(n, away(n)).wait_send()

        @pl.when(jnp.logical_not(same_core(n)))
        def _():
            pass_on(n).wait_send()

        return carry

    lax.fori_loop(0, chunks, given, 0)

    @pl.when(mine)
    def _():
        def shared(k, carry):
            share(k, own_chunk).wait_send()
            return carry

        lax.fori_loop(1, count, shared, 0)

    for d, (dr, dc) in enumerate(SIDES):

        @pl.when(inside(dr, dc))
        def _(d=d):
            copy(d).wait_send()


def whole(feature, mask, dw_weight, dw_bias, ln_gain, ln_bias, w_in, b_in, w_out, b_out, scale, wk, wv, queries, proj):
    nr, nc = lax.axis_size("row"), lax.axis_size("col")
    rows, channels, cols = feature.shape
    hidden = w_in.shape[1]
    positions = rows * cols
    wide = NH * HB
    number = queries.shape[1]
    qb = 256
    chunks = NH * number // 128
    others, chips = nr * nc - 1, nr * nc // 2
    full = pl.BlockSpec(memory_space=pltpu.VMEM)
    return pl.pallas_call(
        functools.partial(whole_kernel, nr, nc),
        out_shape=[
            jax.ShapeDtypeStruct((rows, channels, cols), BF),
            jax.ShapeDtypeStruct((channels, number), F32),
        ],
        in_specs=[full] * 15,
        out_specs=[full] * 2,
        scratch_shapes=[
            pltpu.VMEM((positions, wide), BF),
            pltpu.VMEM((wide, positions), BF),
            pltpu.VMEM((2, 3, channels, cols), BF),
            pltpu.VMEM((2, channels, 128), BF),
            pltpu.VMEM((2, channels, 128), BF),
            pltpu.VMEM((2, 128, channels), BF),
            pltpu.VMEM((128, channels), BF),
            pltpu.VMEM((3, rows * channels, 128), F32),
            pltpu.VMEM((3, 8 * channels, 128), F32),
            pltpu.VMEM((2, rows * channels, 128), F32),
            pltpu.VMEM((128, 256), F32),
            pltpu.VMEM((256, 128), F32),
            pltpu.VMEM((5, channels, 256), F32),
            pltpu.VMEM((channels, hidden), BF),
            pltpu.VMEM((hidden, channels + 16), BF),
            pltpu.VMEM((2 * wide, channels + 16), BF),
            pltpu.VMEM((NH, wide, number), BF),
            pltpu.VMEM((positions, qb), F32),
            pltpu.VMEM((positions, qb), F32),
            pltpu.VMEM((chunks, HB, 128), F32),
            pltpu.VMEM((chunks, HB, 128), F32),
            pltpu.VMEM((chips - 1, HB, 128), F32),
            pltpu.VMEM((wide, number), BF),
            pltpu.VMEM((channels, wide), BF),
            pltpu.SemaphoreType.DMA((8,)),
            pltpu.SemaphoreType.DMA((8,)),
            pltpu.SemaphoreType.DMA((chunks,)),
            pltpu.SemaphoreType.DMA((chunks,)),
            pltpu.SemaphoreType.DMA((chunks,)),
            pltpu.SemaphoreType.DMA((chips - 1,)),
            pltpu.SemaphoreType.DMA((others,)),
            pltpu.SemaphoreType.DMA((chunks,)),
        ],
        compiler_params=pltpu.CompilerParams(
            collective_id=0, has_side_effects=True, vmem_limit_bytes=60 << 20
        ),
        name="whole",
    )(feature, mask, dw_weight, dw_bias, ln_gain, ln_bias, w_in, b_in, w_out, b_out, scale, wk, wv, queries, proj)


def body(
    feature,
    mask,
    dw_weight,
    dw_bias,
    ln_gain,
    ln_bias,
    w_in,
    b_in,
    w_out,
    b_out,
    layer_scale,
    w_key,
    w_value,
    queries,
    w_proj,
):
    block_out, pooled = whole(
        jnp.transpose(feature, (0, 2, 1)),
        mask,
        dw_weight,
        dw_bias,
        ln_gain,
        ln_bias,
        w_in,
        b_in,
        jnp.transpose(w_out),
        b_out,
        layer_scale,
        w_key,
        w_value,
        jnp.transpose(queries),
        w_proj,
    )
    return (jnp.transpose(block_out, (0, 2, 1)), jnp.transpose(pooled))


def solution(mesh):
    return jax.shard_map(
        body,
        mesh=mesh,
        in_specs=(P("row", "col", None), P("row", "col")) + (P(),) * 13,
        out_specs=(P("row", "col", None), P()),
        check_vma=False,
    )
```

```python
import functools
import math

import jax
import jax.numpy as jnp
from jax import lax
from jax.experimental import pallas as pl
from jax.experimental.pallas import tpu as pltpu
from jax.sharding import PartitionSpec as P

NH = 8
HB = 32
LOW = -1e29
MASKED = -1e30
MESH = pl.DeviceIdType.MESH
SIDES = [(0, -1), (0, 1), (-1, 0), (1, 0), (-1, -1), (-1, 1), (1, -1), (1, 1)]
BF, F32 = jnp.bfloat16, jnp.float32


def lanes(shape, axis=1):
    return lax.broadcasted_iota(jnp.int32, shape, axis)


def block_kernel(
    nr,
    nc,
    loads,
    x_ref,
    mask_ref,
    dw_ref,
    dwb_ref,
    gain_ref,
    shift_ref,
    win_ref,
    bin_ref,
    wout_ref,
    bout_ref,
    scale_ref,
    wk_ref,
    wv_ref,
    raw_ref,
    proj_ref,
    out_ref,
    pooled_ref,
    k_ref,
    vt_ref,
    line_ref,
    strip_ref,
    strip_in,
    corner_ref,
    corner_in,
    s_ref,
    z_ref,
    conv_ref,
    tap_ref,
    base_ref,
    col_ref,
    half_ref,
    wint_ref,
    wkv_ref,
    q_ref,
    sa_ref,
    sb_ref,
    part_ref,
    pair_ref,
    inbox,
    gathered,
    projt_ref,
    send,
    recv,
    send_0,
    recv_0,
    send_1,
    recv_1,
    send_2,
    recv_2,
):
    r, c = lax.axis_index("row"), lax.axis_index("col")
    rows, channels, cols = x_ref.shape
    head = channels // NH

    def inside(dr, dc):
        return (r + dr >= 0) & (r + dr < nr) & (c + dc >= 0) & (c + dc < nc)

    me = r * nc + c
    count = nr * nc

    def device(p):
        return (p // nc, lax.rem(p, nc))

    barrier = pltpu.get_barrier_semaphore()

    def greet(k, carry):
        pl.semaphore_signal(
            barrier, inc=1, device_id=device(lax.rem(me + k, count)), device_id_type=MESH
        )
        return carry

    lax.fori_loop(1, count, greet, 0)

    lane = lanes((channels, 128))

    def pack(i, carry):
        low, high = carry
        x = x_ref[i]
        own = (lane >= 8 * i) & (lane < 8 * i + 3)
        low = jnp.where(own, pltpu.roll(x[:, 0:128], 8 * i, 1), low)
        high = jnp.where(own, pltpu.roll(x[:, cols - 128 : cols], 8 * i + 3, 1), high)
        return low, high

    zero = jnp.zeros((channels, 128), F32)
    loads[0].wait()
    edges = lax.fori_loop(0, rows, pack, (zero.astype(BF), zero.astype(BF)))
    for e in range(2):
        strip_ref[e] = edges[e]
        corner_ref[e] = jnp.transpose(edges[e].astype(F32)).astype(BF)

    pl.semaphore_wait(barrier, count - 1)

    def copy(d):
        dr, dc = SIDES[d]
        if dr == 0:
            src = strip_ref.at[0 if dc < 0 else 1]
            dst = strip_in.at[1 if dc < 0 else 0]
        elif dc == 0:
            src = x_ref.at[pl.ds(0 if dr < 0 else rows - 3, 3)]
            dst = line_ref.at[1 if dr < 0 else 0]
        else:
            src = corner_ref.at[0 if dc < 0 else 1, pl.ds(0 if dr < 0 else 96, 32)]
            dst = corner_in.at[pl.ds((64 if dc < 0 else 0) + (32 if dr < 0 else 0), 32)]
        return pltpu.make_async_remote_copy(
            src_ref=src,
            dst_ref=dst,
            send_sem=send.at[d],
            recv_sem=recv.at[d],
            device_id=(r + dr, c + dc),
            device_id_type=MESH,
        )

    for d, (dr, dc) in enumerate(SIDES):

        @pl.when(inside(dr, dc))
        def _(d=d):
            copy(d).start()

        @pl.when(jnp.logical_not(inside(-dr, -dc)))
        def _(d=d, dr=dr, dc=dc):
            if dr == 0:
                strip_in[1 if dc < 0 else 0] = jnp.zeros((channels, 128), BF)
            elif dc == 0:
                line_ref[1 if dr < 0 else 0] = jnp.zeros((3, channels, cols), BF)
            else:
                at = (64 if dc < 0 else 0) + (32 if dr < 0 else 0)
                corner_in[at : at + 32] = jnp.zeros((32, channels), BF)

    for load in loads[1:]:
        load.wait()

    tap_ref[...] = jnp.zeros_like(tap_ref)
    for a in range(7):
        for b in range(7):
            at = (b * 16 + a - 3) % 128
            tap_ref[at : at + 1, 0:channels] = dw_ref[a, b : b + 1, :]
    base_ref[...] = jnp.transpose(tap_ref[...])

    def column(vector, size):
        wide = jnp.broadcast_to(vector[None, :], (128, size))
        return jnp.transpose(wide)

    for n, ref in enumerate((dwb_ref, gain_ref, shift_ref, bout_ref, scale_ref)):
        wide = column(ref[...], channels)
        col_ref[n, :, 0:128] = wide
        col_ref[n, :, 128:256] = wide
    level = jnp.broadcast_to(bin_ref[...][None, :], (8, bin_ref.shape[0]))
    row8 = lanes(level.shape, 0)
    terms = jnp.zeros_like(level)
    for n in range(3):
        term = level.astype(BF).astype(F32)
        terms = jnp.where(row8 == n, term, terms)
        level = level - term
    stack = jnp.concatenate([win_ref[...].astype(F32), terms, jnp.zeros_like(terms)], axis=0)
    wint_ref[...] = jnp.transpose(stack).astype(BF)
    half_ref[...] = (wout_ref[...].astype(F32) * 0.5).astype(BF)
    pad = jnp.zeros((HB - head, channels), F32)
    mark_row, mark_lane = lanes((HB, 16), 0), lanes((HB, 16), 1)
    for n, ref in enumerate((wk_ref, wv_ref)):
        turned = jnp.transpose(ref[...].astype(F32))
        for h in range(NH):
            piece = jnp.concatenate([turned[h * head : (h + 1) * head], pad], axis=0)
            tag = 1.0 if n == 1 else (1.0 if h == 0 else 0.0)
            mark = jnp.where((mark_row == head) & (mark_lane == (0 if n == 1 else 1)), tag, 0.0)
            at = n * NH * HB + h * HB
            wkv_ref[at : at + HB, :] = jnp.concatenate([piece, mark], axis=1).astype(BF)

    turned = []
    proj = proj_ref[...].astype(F32)
    for h in range(NH):
        turned += [proj[h * head : (h + 1) * head], pad]
    projt_ref[...] = jnp.transpose(jnp.concatenate(turned, axis=0)).astype(BF)
    queries = raw_ref.shape[1]
    raw = raw_ref[...].astype(F32)
    one = jnp.where(lanes((HB - head, queries), 0) == 0, 1.0, 0.0)
    for h in range(NH):
        q_ref[h] = jnp.zeros((NH * HB, queries), BF)
        if h > 0:
            q_ref[h, 16:32] = jnp.concatenate([jnp.zeros((8, queries), F32), one], axis=0).astype(BF)
        own = jnp.concatenate([raw[h * head : (h + 1) * head], one if h == 0 else one * 0.0], axis=0)
        q_ref[h, h * HB : (h + 1) * HB] = own.astype(BF)

    def widen(i, carry):
        x = x_ref[i].astype(F32)
        at = pl.multiple_of(i * channels, channels)
        s_ref[0, pl.ds(at, channels)] = x[:, 0:128]
        s_ref[1, pl.ds(at, channels)] = x[:, 128:256]
        return carry

    lax.fori_loop(0, rows, widen, 0)

    def land(d):
        dr, dc = SIDES[d]

        @pl.when(inside(-dr, -dc))
        def _():
            copy(d).wait_recv()

    land(0)
    land(1)

    def side(low, high):
        return jnp.where(lane < 3, low, jnp.where(lane >= 125, high, 0.0))

    def unpack(i, carry):
        left = pltpu.roll(strip_in[0], 125 + (128 - 8 * i), 1).astype(F32)
        right = pltpu.roll(strip_in[1], 128 - 8 * i, 1).astype(F32)
        at = pl.multiple_of(i * channels, channels)
        s_ref[2, pl.ds(at, channels)] = side(right, left)
        return carry

    lax.fori_loop(0, rows, unpack, 0)

    out_row = lanes((rows, 128), 0)
    in_row = lanes((rows, 128), 1) % 16
    near = (in_row - out_row <= 3) & (out_row - in_row <= 3)

    def bands(ch, keep):
        tap = jnp.broadcast_to(base_ref[pl.ds(ch, 1), :], (rows, 128))
        band = jnp.where(keep, pltpu.roll(tap, 0, 1, stride=1, stride_axis=0), 0.0)
        high = band.astype(BF)
        low = (band - high.astype(F32)).astype(BF)
        return jnp.concatenate([high, low], axis=0)

    UN = 48

    def local(step, carry):
        for u in range(UN):
            ch = step * UN + u
            x = jnp.concatenate(
                [s_ref[t, pl.ds(ch, rows, stride=channels), :] for t in range(3)], axis=1
            ).astype(BF)
            parts = [pltpu.roll(x, (3 - b) % 384, 1)[:, 0:cols] for b in range(7)]
            band = bands(ch, near)
            y = jnp.dot(
                band[:, 0:112], jnp.concatenate(parts, axis=0), preferred_element_type=F32
            )
            y = y[0:rows] + y[rows : 2 * rows]
            at = pl.multiple_of(ch * rows, rows)
            conv_ref[0, pl.ds(at, rows)] = y[:, 0:128]
            conv_ref[1, pl.ds(at, rows)] = y[:, 128:256]
        return carry

    lax.fori_loop(0, channels // UN, local, 0)

    row16 = lanes((16, cols), 0)
    ones16 = jnp.where(row16 < 3, 1.0, 0.0).astype(BF)

    def norm(row):
        flat = jnp.concatenate(
            [conv_ref[t, pl.ds(row, channels, stride=rows), :] for t in range(2)], axis=1
        )
        flat = flat + col_ref[0]
        average = jnp.sum(flat, axis=0, keepdims=True) * (1.0 / channels)
        moved = flat - average
        spread = jnp.sum(moved * moved, axis=0, keepdims=True) * (1.0 / channels)
        normed = (moved * lax.rsqrt(spread + 1e-06) * col_ref[1] + col_ref[2]).astype(BF)
        return jnp.concatenate([normed, ones16], axis=0)

    def expand(normed):
        inner = jnp.dot(wint_ref[...], normed, preferred_element_type=F32)
        return (inner * (1.0 + lax.erf(inner * math.sqrt(0.5)))).astype(BF)

    def contract(row, act):
        branch = jnp.dot(half_ref[...], act, preferred_element_type=F32) + col_ref[3]
        result = (x_ref[row].astype(F32) + col_ref[4] * branch).astype(BF)
        out_ref[row] = result
        bias = jnp.where(mask_ref[pl.ds(row, 1), :] > 0, 0.0, MASKED)
        extra = jnp.where(row16 == 0, 1.0, jnp.where(row16 == 1, bias, 0.0)).astype(BF)
        result = jnp.concatenate([result, extra], axis=0)
        both = jnp.dot(wkv_ref[...], result, preferred_element_type=F32)
        keys, values = both[0 : NH * HB], both[NH * HB : 2 * NH * HB]
        at = pl.multiple_of(row * cols, cols)
        k_ref[pl.ds(at, cols), :] = jnp.transpose(keys).astype(BF)
        vt_ref[:, pl.ds(at, cols)] = values.astype(BF)

    def mlp(numbers):
        size = len(numbers)
        normed, act = {}, {}
        for n in range(size + 2):
            if n < size:
                normed[n] = norm(numbers[n])
            if 0 <= n - 1 < size:
                act[n - 1] = expand(normed.pop(n - 1))
            if 0 <= n - 2:
                contract(numbers[n - 2], act.pop(n - 2))

    mlp(list(range(3, rows - 3)))

    for d in range(2, 8):
        land(d)

    turned = jnp.transpose(corner_in[...].astype(F32))
    for s in range(8):
        at = s * channels
        if s < 3:
            line = line_ref[1, s].astype(F32)
            right, left = 96 + 8 * s, 32 + 8 * s
        elif s > 4:
            line = line_ref[0, s - 5].astype(F32)
            right, left = 64 + 8 * (s - 4), 8 * (s - 4)
        else:
            for t in range(3):
                z_ref[t, at : at + channels] = zero
            continue
        z_ref[0, at : at + channels] = line[:, 0:128]
        z_ref[1, at : at + channels] = line[:, 128:256]
        z_ref[2, at : at + channels] = side(
            pltpu.roll(turned, 128 - right, 1), pltpu.roll(turned, (125 - left) % 128, 1)
        )

    far = jnp.logical_not(near)

    def outer(step, carry):
        for u in range(UN):
            ch = step * UN + u
            x = jnp.concatenate(
                [z_ref[t, pl.ds(ch, 8, stride=channels), :] for t in range(3)], axis=1
            )
            parts = [pltpu.roll(x, (3 - b) % 384, 1)[:, 0:cols] for b in range(7)]
            groups = []
            for g in range(8):
                groups += [parts[max(g - 1, 0)], parts[(g + 1) % 8 if g != 6 else 0]]
            band = bands(ch, far)
            y = jnp.dot(
                band, jnp.concatenate(groups, axis=0).astype(BF), preferred_element_type=F32
            )
            y = y[0:rows] + y[rows : 2 * rows]
            at = pl.multiple_of(ch * rows, rows)
            conv_ref[0, pl.ds(at, rows)] += y[:, 0:128]
            conv_ref[1, pl.ds(at, rows)] += y[:, 128:256]
        return carry

    lax.fori_loop(0, channels // UN, outer, 0)

    mlp([0, 1, 2, rows - 3, rows - 2, rows - 1])

    qb = sa_ref.shape[1]
    blocks = queries // qb
    total = NH * blocks
    factor = math.log2(math.e) / math.sqrt(head)
    per = qb // 128
    chunks = total * per
    stride = count // chunks
    row = lanes((HB, qb), 0)

    def owner(n):
        return lax.rem(n * 11 + 31, chunks) * stride

    mine = lax.rem(me, stride) == 0
    own_chunk = lax.rem((me // stride + 1) * 3, chunks)

    def place(index):
        h = index // blocks
        return h, pl.multiple_of((index - h * blocks) * qb, qb)

    def score(index, s_ref):
        h, at = place(index)
        s = jnp.dot(k_ref[...], q_ref[h, :, pl.ds(at, qb)], preferred_element_type=F32)
        s_ref[...] = s
        return jnp.maximum(jnp.max(s, axis=0, keepdims=True), LOW)

    def absorb(index, s_ref, top):
        h, at = place(index)
        e = jnp.exp2((s_ref[...] - top) * factor).astype(BF)
        v = vt_ref[pl.ds(pl.multiple_of(h * HB, HB), HB), :]
        o = jnp.dot(v, e, preferred_element_type=F32)
        o = jnp.where(row == head + 1, top * factor, o)
        for n in range(per):
            part_ref[index * per + n] = o[:, n * 128 : n * 128 + 128]

    chip, core = me // 2, lax.rem(me, 2)
    chips = count // 2

    def pass_on(n):
        return pltpu.make_async_remote_copy(
            src_ref=part_ref.at[n],
            dst_ref=pair_ref.at[n],
            send_sem=send_0.at[n],
            recv_sem=recv_0.at[n],
            device_id=device(chip * 2 + 1 - core),
            device_id_type=MESH,
        )

    def give(n, k):
        return pltpu.make_async_remote_copy(
            src_ref=part_ref.at[n],
            dst_ref=inbox.at[k - 1],
            send_sem=send_1.at[n],
            recv_sem=recv_1.at[k - 1],
            device_id=device(owner(n)),
            device_id_type=MESH,
        )

    def away(n):
        return lax.rem(owner(n) // 2 - chip + chips, chips)

    def same_core(n):
        return lax.rem(owner(n), 2) == core

    def chunk_of(n):
        h = n // (blocks * per)
        at = pl.multiple_of((n - h * blocks * per) * 128, 128)
        return gathered.at[pl.ds(pl.multiple_of(h * HB, HB), HB), pl.ds(at, 128)]

    def share(k, n):
        return pltpu.make_async_remote_copy(
            src_ref=chunk_of(n),
            dst_ref=chunk_of(n),
            send_sem=send_2.at[k - 1],
            recv_sem=recv_2.at[n],
            device_id=device(lax.rem(me + k, count)),
            device_id_type=MESH,
        )

    row1 = lanes((HB, 128), 0)

    def hand_over(pair):
        for n in range(2 * per):
            chunk = pair * 2 * per + n

            @pl.when(jnp.logical_not(same_core(chunk)))
            def _(chunk=chunk):
                pass_on(chunk).start()

    def hand_out(pair):
        for n in range(2 * per):
            chunk = pair * 2 * per + n

            @pl.when(same_core(chunk))
            def _(chunk=chunk):
                pass_on(chunk).wait_recv()
                one, two = part_ref[chunk], pair_ref[chunk]
                first, second = one[head + 1 : head + 2], two[head + 1 : head + 2]
                top = jnp.maximum(first, second)
                both = one * jnp.exp2(first - top) + two * jnp.exp2(second - top)
                part_ref[chunk] = jnp.where(row1 == head + 1, top, both)

                @pl.when(owner(chunk) != me)
                def _():
                    give(chunk, away(chunk)).start()

    def finish():
        def arrive(k, carry):
            give(own_chunk, k).wait_recv()
            return carry

        lax.fori_loop(1, chips, arrive, 0)
        piece = part_ref[own_chunk]
        level = piece[head + 1 : head + 2]

        def highest(k, top):
            return jnp.maximum(top, inbox[k - 1, head + 1 : head + 2, :])

        top = lax.fori_loop(1, chips, highest, level)

        def add(k, total):
            piece = inbox[k - 1]
            return total + piece * jnp.exp2(piece[head + 1 : head + 2] - top)

        summed = lax.fori_loop(1, chips, add, piece * jnp.exp2(level - top))
        pooled = jnp.where(row1 < head, summed / summed[head : head + 1], 0.0)
        chunk_of(own_chunk)[...] = pooled.astype(BF)

        def share_start(k, carry):
            share(k, own_chunk).start()
            return carry

        lax.fori_loop(1, count, share_start, 0)

    LAG = 4
    own_pair = own_chunk // (2 * per)
    top_a = score(0, sa_ref)

    def attend(pair, top_a):
        index = pair * 2
        top_b = score(index + 1, sb_ref)
        absorb(index, sa_ref, top_a)
        top_a = score(index + 2, sa_ref)
        absorb(index + 1, sb_ref, top_b)
        hand_over(pair)

        @pl.when(pair > 0)
        def _():
            hand_out(pair - 1)

        @pl.when(mine & (own_pair + LAG == pair))
        def _():
            finish()

        return top_a

    pairs = total // 2
    top_a = lax.fori_loop(0, pairs - 1, attend, top_a)
    top_b = score(total - 1, sb_ref)
    absorb(total - 2, sa_ref, top_a)
    absorb(total - 1, sb_ref, top_b)
    hand_over(pairs - 1)
    hand_out(pairs - 2)
    hand_out(pairs - 1)

    @pl.when(mine & (own_pair + LAG >= pairs - 1))
    def _():
        finish()

    def collect(n, carry):
        @pl.when(owner(n) != me)
        def _():
            share(1, n).wait_recv()

        return carry

    lax.fori_loop(0, chunks, collect, 0)
    pooled_ref[...] = jnp.dot(projt_ref[...], gathered[...], preferred_element_type=F32)

    def given(n, carry):
        @pl.when(same_core(n) & (owner(n) != me))
        def _():
            give(n, away(n)).wait_send()

        @pl.when(jnp.logical_not(same_core(n)))
        def _():
            pass_on(n).wait_send()

        return carry

    lax.fori_loop(0, chunks, given, 0)

    @pl.when(mine)
    def _():
        def shared(k, carry):
            share(k, own_chunk).wait_send()
            return carry

        lax.fori_loop(1, count, shared, 0)

    for d, (dr, dc) in enumerate(SIDES):

        @pl.when(inside(dr, dc))
        def _(d=d):
            copy(d).wait_send()


def whole_kernel(nr, nc, number, *refs):
    given, outs, held = refs[:number], refs[number : number + 2], refs[number + 2 : 2 * number + 2]
    sems, rest = refs[2 * number + 2], refs[2 * number + 3 :]
    loads = [pltpu.make_async_copy(given[n], held[n], sems.at[n]) for n in range(number)]
    for load in loads:
        load.start()
    block_kernel(nr, nc, loads, *held, *outs, *rest)


def whole(feature, mask, dw_weight, dw_bias, ln_gain, ln_bias, w_in, b_in, w_out, b_out, scale, wk, wv, queries, proj):
    nr, nc = lax.axis_size("row"), lax.axis_size("col")
    rows, channels, cols = feature.shape
    hidden = w_in.shape[1]
    positions = rows * cols
    wide = NH * HB
    number = queries.shape[1]
    qb = 256
    chunks = NH * number // 128
    others, chips = nr * nc - 1, nr * nc // 2
    full = pl.BlockSpec(memory_space=pltpu.VMEM)
    args = (feature, mask, dw_weight, dw_bias, ln_gain, ln_bias, w_in, b_in, w_out, b_out, scale, wk, wv, queries, proj)
    return pl.pallas_call(
        functools.partial(whole_kernel, nr, nc, len(args)),
        out_shape=[
            jax.ShapeDtypeStruct((rows, channels, cols), BF),
            jax.ShapeDtypeStruct((channels, number), F32),
        ],
        in_specs=[pl.BlockSpec(memory_space=pltpu.HBM)] * len(args),
        out_specs=[full] * 2,
        scratch_shapes=[pltpu.VMEM(a.shape, a.dtype) for a in args]
        + [
            pltpu.SemaphoreType.DMA((len(args),)),
            pltpu.VMEM((positions, wide), BF),
            pltpu.VMEM((wide, positions), BF),
            pltpu.VMEM((2, 3, channels, cols), BF),
            pltpu.VMEM((2, channels, 128), BF),
            pltpu.VMEM((2, channels, 128), BF),
            pltpu.VMEM((2, 128, channels), BF),
            pltpu.VMEM((128, channels), BF),
            pltpu.VMEM((3, rows * channels, 128), F32),
            pltpu.VMEM((3, 8 * channels, 128), F32),
            pltpu.VMEM((2, rows * channels, 128), F32),
            pltpu.VMEM((128, 256), F32),
            pltpu.VMEM((256, 128), F32),
            pltpu.VMEM((5, channels, 256), F32),
            pltpu.VMEM((channels, hidden), BF),
            pltpu.VMEM((hidden, channels + 16), BF),
            pltpu.VMEM((2 * wide, channels + 16), BF),
            pltpu.VMEM((NH, wide, number), BF),
            pltpu.VMEM((positions, qb), F32),
            pltpu.VMEM((positions, qb), F32),
            pltpu.VMEM((chunks, HB, 128), F32),
            pltpu.VMEM((chunks, HB, 128), F32),
            pltpu.VMEM((chips - 1, HB, 128), F32),
            pltpu.VMEM((wide, number), BF),
            pltpu.VMEM((channels, wide), BF),
            pltpu.SemaphoreType.DMA((8,)),
            pltpu.SemaphoreType.DMA((8,)),
            pltpu.SemaphoreType.DMA((chunks,)),
            pltpu.SemaphoreType.DMA((chunks,)),
            pltpu.SemaphoreType.DMA((chunks,)),
            pltpu.SemaphoreType.DMA((chips - 1,)),
            pltpu.SemaphoreType.DMA((others,)),
            pltpu.SemaphoreType.DMA((chunks,)),
        ],
        compiler_params=pltpu.CompilerParams(
            collective_id=0, has_side_effects=True, vmem_limit_bytes=60 << 20
        ),
        name="whole",
    )(*args)


def body(
    feature,
    mask,
    dw_weight,
    dw_bias,
    ln_gain,
    ln_bias,
    w_in,
    b_in,
    w_out,
    b_out,
    layer_scale,
    w_key,
    w_value,
    queries,
    w_proj,
):
    block_out, pooled = whole(
        jnp.transpose(feature, (0, 2, 1)),
        mask,
        dw_weight,
        dw_bias,
        ln_gain,
        ln_bias,
        w_in,
        b_in,
        jnp.transpose(w_out),
        b_out,
        layer_scale,
        w_key,
        w_value,
        jnp.transpose(queries),
        w_proj,
    )
    return (jnp.transpose(block_out, (0, 2, 1)), jnp.transpose(pooled))


def solution(mesh):
    return jax.shard_map(
        body,
        mesh=mesh,
        in_specs=(P("row", "col", None), P("row", "col")) + (P(),) * 13,
        out_specs=(P("row", "col", None), P()),
        check_vma=False,
    )
```

```python
import functools
import math

import jax
import jax.numpy as jnp
from jax import lax
from jax.experimental import pallas as pl
from jax.experimental.pallas import tpu as pltpu
from jax.sharding import PartitionSpec as P

NH = 8
HB = 32
LOW = -1e29
MASKED = -1e30
MESH = pl.DeviceIdType.MESH
SIDES = [(0, -1), (0, 1), (-1, 0), (1, 0), (-1, -1), (-1, 1), (1, -1), (1, 1)]
BF, F32 = jnp.bfloat16, jnp.float32


def lanes(shape, axis=1):
    return lax.broadcasted_iota(jnp.int32, shape, axis)


def block_kernel(
    nr,
    nc,
    loads,
    x_ref,
    mask_ref,
    dw_ref,
    dwb_ref,
    gain_ref,
    shift_ref,
    win_ref,
    bin_ref,
    wout_ref,
    bout_ref,
    scale_ref,
    wk_ref,
    wv_ref,
    raw_ref,
    proj_ref,
    out_hbm,
    pooled_ref,
    out_ref,
    out_sem,
    k_ref,
    vt_ref,
    line_ref,
    strip_ref,
    strip_in,
    corner_ref,
    corner_in,
    s_ref,
    z_ref,
    conv_ref,
    tap_ref,
    base_ref,
    col_ref,
    half_ref,
    wint_ref,
    wkv_ref,
    q_ref,
    sa_ref,
    sb_ref,
    part_ref,
    pair_ref,
    inbox,
    gathered,
    projt_ref,
    send,
    recv,
    send_0,
    recv_0,
    send_1,
    recv_1,
    send_2,
    recv_2,
):
    r, c = lax.axis_index("row"), lax.axis_index("col")
    rows, channels, cols = x_ref.shape
    head = channels // NH

    def inside(dr, dc):
        return (r + dr >= 0) & (r + dr < nr) & (c + dc >= 0) & (c + dc < nc)

    me = r * nc + c
    count = nr * nc

    def device(p):
        return (p // nc, lax.rem(p, nc))

    barrier = pltpu.get_barrier_semaphore()

    def greet(k, carry):
        pl.semaphore_signal(
            barrier, inc=1, device_id=device(lax.rem(me + k, count)), device_id_type=MESH
        )
        return carry

    lax.fori_loop(1, count, greet, 0)

    lane = lanes((channels, 128))

    def pack(i, carry):
        low, high = carry
        x = x_ref[i]
        own = (lane >= 8 * i) & (lane < 8 * i + 3)
        low = jnp.where(own, pltpu.roll(x[:, 0:128], 8 * i, 1), low)
        high = jnp.where(own, pltpu.roll(x[:, cols - 128 : cols], 8 * i + 3, 1), high)
        return low, high

    zero = jnp.zeros((channels, 128), F32)
    loads[0].wait()
    edges = lax.fori_loop(0, rows, pack, (zero.astype(BF), zero.astype(BF)))
    for e in range(2):
        strip_ref[e] = edges[e]
        corner_ref[e] = jnp.transpose(edges[e].astype(F32)).astype(BF)

    pl.semaphore_wait(barrier, count - 1)

    def copy(d):
        dr, dc = SIDES[d]
        if dr == 0:
            src = strip_ref.at[0 if dc < 0 else 1]
            dst = strip_in.at[1 if dc < 0 else 0]
        elif dc == 0:
            src = x_ref.at[pl.ds(0 if dr < 0 else rows - 3, 3)]
            dst = line_ref.at[1 if dr < 0 else 0]
        else:
            src = corner_ref.at[0 if dc < 0 else 1, pl.ds(0 if dr < 0 else 96, 32)]
            dst = corner_in.at[pl.ds((64 if dc < 0 else 0) + (32 if dr < 0 else 0), 32)]
        return pltpu.make_async_remote_copy(
            src_ref=src,
            dst_ref=dst,
            send_sem=send.at[d],
            recv_sem=recv.at[d],
            device_id=(r + dr, c + dc),
            device_id_type=MESH,
        )

    for d, (dr, dc) in enumerate(SIDES):

        @pl.when(inside(dr, dc))
        def _(d=d):
            copy(d).start()

        @pl.when(jnp.logical_not(inside(-dr, -dc)))
        def _(d=d, dr=dr, dc=dc):
            if dr == 0:
                strip_in[1 if dc < 0 else 0] = jnp.zeros((channels, 128), BF)
            elif dc == 0:
                line_ref[1 if dr < 0 else 0] = jnp.zeros((3, channels, cols), BF)
            else:
                at = (64 if dc < 0 else 0) + (32 if dr < 0 else 0)
                corner_in[at : at + 32] = jnp.zeros((32, channels), BF)

    for load in loads[1:]:
        load.wait()

    tap_ref[...] = jnp.zeros_like(tap_ref)
    for a in range(7):
        for b in range(7):
            at = (b * 16 + a - 3) % 128
            tap_ref[at : at + 1, 0:channels] = dw_ref[a, b : b + 1, :]
    base_ref[...] = jnp.transpose(tap_ref[...])

    def column(vector, size):
        wide = jnp.broadcast_to(vector[None, :], (128, size))
        return jnp.transpose(wide)

    for n, ref in enumerate((dwb_ref, gain_ref, shift_ref, bout_ref, scale_ref)):
        wide = column(ref[...], channels)
        col_ref[n, :, 0:128] = wide
        col_ref[n, :, 128:256] = wide
    level = jnp.broadcast_to(bin_ref[...][None, :], (8, bin_ref.shape[0]))
    row8 = lanes(level.shape, 0)
    terms = jnp.zeros_like(level)
    for n in range(3):
        term = level.astype(BF).astype(F32)
        terms = jnp.where(row8 == n, term, terms)
        level = level - term
    stack = jnp.concatenate([win_ref[...].astype(F32), terms, jnp.zeros_like(terms)], axis=0)
    wint_ref[...] = jnp.transpose(stack).astype(BF)
    half_ref[...] = (wout_ref[...].astype(F32) * 0.5).astype(BF)
    pad = jnp.zeros((HB - head, channels), F32)
    mark_row, mark_lane = lanes((HB, 16), 0), lanes((HB, 16), 1)
    for n, ref in enumerate((wk_ref, wv_ref)):
        turned = jnp.transpose(ref[...].astype(F32))
        for h in range(NH):
            piece = jnp.concatenate([turned[h * head : (h + 1) * head], pad], axis=0)
            tag = 1.0 if n == 1 else (1.0 if h == 0 else 0.0)
            mark = jnp.where((mark_row == head) & (mark_lane == (0 if n == 1 else 1)), tag, 0.0)
            at = n * NH * HB + h * HB
            wkv_ref[at : at + HB, :] = jnp.concatenate([piece, mark], axis=1).astype(BF)

    turned = []
    proj = proj_ref[...].astype(F32)
    for h in range(NH):
        turned += [proj[h * head : (h + 1) * head], pad]
    projt_ref[...] = jnp.transpose(jnp.concatenate(turned, axis=0)).astype(BF)
    queries = raw_ref.shape[1]
    raw = raw_ref[...].astype(F32)
    one = jnp.where(lanes((HB - head, queries), 0) == 0, 1.0, 0.0)
    for h in range(NH):
        q_ref[h] = jnp.zeros((NH * HB, queries), BF)
        if h > 0:
            q_ref[h, 16:32] = jnp.concatenate([jnp.zeros((8, queries), F32), one], axis=0).astype(BF)
        own = jnp.concatenate([raw[h * head : (h + 1) * head], one if h == 0 else one * 0.0], axis=0)
        q_ref[h, h * HB : (h + 1) * HB] = own.astype(BF)

    def widen(i, carry):
        x = x_ref[i].astype(F32)
        at = pl.multiple_of(i * channels, channels)
        s_ref[0, pl.ds(at, channels)] = x[:, 0:128]
        s_ref[1, pl.ds(at, channels)] = x[:, 128:256]
        return carry

    lax.fori_loop(0, rows, widen, 0)

    def land(d):
        dr, dc = SIDES[d]

        @pl.when(inside(-dr, -dc))
        def _():
            copy(d).wait_recv()

    land(0)
    land(1)

    def side(low, high):
        return jnp.where(lane < 3, low, jnp.where(lane >= 125, high, 0.0))

    def unpack(i, carry):
        left = pltpu.roll(strip_in[0], 125 + (128 - 8 * i), 1).astype(F32)
        right = pltpu.roll(strip_in[1], 128 - 8 * i, 1).astype(F32)
        at = pl.multiple_of(i * channels, channels)
        s_ref[2, pl.ds(at, channels)] = side(right, left)
        return carry

    lax.fori_loop(0, rows, unpack, 0)

    out_row = lanes((rows, 128), 0)
    in_row = lanes((rows, 128), 1) % 16
    near = (in_row - out_row <= 3) & (out_row - in_row <= 3)

    def bands(ch, keep):
        tap = jnp.broadcast_to(base_ref[pl.ds(ch, 1), :], (rows, 128))
        band = jnp.where(keep, pltpu.roll(tap, 0, 1, stride=1, stride_axis=0), 0.0)
        high = band.astype(BF)
        low = (band - high.astype(F32)).astype(BF)
        return jnp.concatenate([high, low], axis=0)

    UN = 48

    def local(step, carry):
        for u in range(UN):
            ch = step * UN + u
            x = jnp.concatenate(
                [s_ref[t, pl.ds(ch, rows, stride=channels), :] for t in range(3)], axis=1
            ).astype(BF)
            parts = [pltpu.roll(x, (3 - b) % 384, 1)[:, 0:cols] for b in range(7)]
            band = bands(ch, near)
            y = jnp.dot(
                band[:, 0:112], jnp.concatenate(parts, axis=0), preferred_element_type=F32
            )
            y = y[0:rows] + y[rows : 2 * rows]
            at = pl.multiple_of(ch * rows, rows)
            conv_ref[0, pl.ds(at, rows)] = y[:, 0:128]
            conv_ref[1, pl.ds(at, rows)] = y[:, 128:256]
        return carry

    lax.fori_loop(0, channels // UN, local, 0)

    row16 = lanes((16, cols), 0)
    ones16 = jnp.where(row16 < 3, 1.0, 0.0).astype(BF)

    def norm(row):
        flat = jnp.concatenate(
            [conv_ref[t, pl.ds(row, channels, stride=rows), :] for t in range(2)], axis=1
        )
        flat = flat + col_ref[0]
        average = jnp.sum(flat, axis=0, keepdims=True) * (1.0 / channels)
        moved = flat - average
        spread = jnp.sum(moved * moved, axis=0, keepdims=True) * (1.0 / channels)
        normed = (moved * lax.rsqrt(spread + 1e-06) * col_ref[1] + col_ref[2]).astype(BF)
        return jnp.concatenate([normed, ones16], axis=0)

    def expand(normed):
        inner = jnp.dot(wint_ref[...], normed, preferred_element_type=F32)
        return (inner * (1.0 + lax.erf(inner * math.sqrt(0.5)))).astype(BF)

    def contract(row, act):
        branch = jnp.dot(half_ref[...], act, preferred_element_type=F32) + col_ref[3]
        result = (x_ref[row].astype(F32) + col_ref[4] * branch).astype(BF)
        out_ref[row] = result
        bias = jnp.where(mask_ref[pl.ds(row, 1), :] > 0, 0.0, MASKED)
        extra = jnp.where(row16 == 0, 1.0, jnp.where(row16 == 1, bias, 0.0)).astype(BF)
        result = jnp.concatenate([result, extra], axis=0)
        both = jnp.dot(wkv_ref[...], result, preferred_element_type=F32)
        keys, values = both[0 : NH * HB], both[NH * HB : 2 * NH * HB]
        at = pl.multiple_of(row * cols, cols)
        k_ref[pl.ds(at, cols), :] = jnp.transpose(keys).astype(BF)
        vt_ref[:, pl.ds(at, cols)] = values.astype(BF)

    def mlp(numbers):
        size = len(numbers)
        normed, act = {}, {}
        for n in range(size + 2):
            if n < size:
                normed[n] = norm(numbers[n])
            if 0 <= n - 1 < size:
                act[n - 1] = expand(normed.pop(n - 1))
            if 0 <= n - 2:
                contract(numbers[n - 2], act.pop(n - 2))

    mlp(list(range(3, rows - 3)))

    for d in range(2, 8):
        land(d)

    turned = jnp.transpose(corner_in[...].astype(F32))
    for s in range(8):
        at = s * channels
        if s < 3:
            line = line_ref[1, s].astype(F32)
            right, left = 96 + 8 * s, 32 + 8 * s
        elif s > 4:
            line = line_ref[0, s - 5].astype(F32)
            right, left = 64 + 8 * (s - 4), 8 * (s - 4)
        else:
            for t in range(3):
                z_ref[t, at : at + channels] = zero
            continue
        z_ref[0, at : at + channels] = line[:, 0:128]
        z_ref[1, at : at + channels] = line[:, 128:256]
        z_ref[2, at : at + channels] = side(
            pltpu.roll(turned, 128 - right, 1), pltpu.roll(turned, (125 - left) % 128, 1)
        )

    far = jnp.logical_not(near)

    def outer(step, carry):
        for u in range(UN):
            ch = step * UN + u
            x = jnp.concatenate(
                [z_ref[t, pl.ds(ch, 8, stride=channels), :] for t in range(3)], axis=1
            )
            parts = [pltpu.roll(x, (3 - b) % 384, 1)[:, 0:cols] for b in range(7)]
            groups = []
            for g in range(8):
                groups += [parts[max(g - 1, 0)], parts[(g + 1) % 8 if g != 6 else 0]]
            band = bands(ch, far)
            y = jnp.dot(
                band, jnp.concatenate(groups, axis=0).astype(BF), preferred_element_type=F32
            )
            y = y[0:rows] + y[rows : 2 * rows]
            at = pl.multiple_of(ch * rows, rows)
            conv_ref[0, pl.ds(at, rows)] += y[:, 0:128]
            conv_ref[1, pl.ds(at, rows)] += y[:, 128:256]
        return carry

    lax.fori_loop(0, channels // UN, outer, 0)

    mlp([0, 1, 2, rows - 3, rows - 2, rows - 1])

    keep = pltpu.make_async_copy(out_ref, out_hbm, out_sem)
    keep.start()

    qb = sa_ref.shape[1]
    blocks = queries // qb
    total = NH * blocks
    factor = math.log2(math.e) / math.sqrt(head)
    per = qb // 128
    chunks = total * per
    stride = count // chunks
    row = lanes((HB, qb), 0)

    def owner(n):
        return lax.rem(n * 11 + 31, chunks) * stride

    mine = lax.rem(me, stride) == 0
    own_chunk = lax.rem((me // stride + 1) * 3, chunks)

    def place(index):
        h = index // blocks
        return h, pl.multiple_of((index - h * blocks) * qb, qb)

    def score(index, s_ref):
        h, at = place(index)
        s = jnp.dot(k_ref[...], q_ref[h, :, pl.ds(at, qb)], preferred_element_type=F32)
        s_ref[...] = s
        return jnp.maximum(jnp.max(s, axis=0, keepdims=True), LOW)

    def absorb(index, s_ref, top):
        h, at = place(index)
        e = jnp.exp2((s_ref[...] - top) * factor).astype(BF)
        v = vt_ref[pl.ds(pl.multiple_of(h * HB, HB), HB), :]
        o = jnp.dot(v, e, preferred_element_type=F32)
        o = jnp.where(row == head + 1, top * factor, o)
        for n in range(per):
            part_ref[index * per + n] = o[:, n * 128 : n * 128 + 128]

    chip, core = me // 2, lax.rem(me, 2)
    chips = count // 2

    def pass_on(n):
        return pltpu.make_async_remote_copy(
            src_ref=part_ref.at[n],
            dst_ref=pair_ref.at[n],
            send_sem=send_0.at[n],
            recv_sem=recv_0.at[n],
            device_id=device(chip * 2 + 1 - core),
            device_id_type=MESH,
        )

    def give(n, k):
        return pltpu.make_async_remote_copy(
            src_ref=part_ref.at[n],
            dst_ref=inbox.at[k - 1],
            send_sem=send_1.at[n],
            recv_sem=recv_1.at[k - 1],
            device_id=device(owner(n)),
            device_id_type=MESH,
        )

    def away(n):
        return lax.rem(owner(n) // 2 - chip + chips, chips)

    def same_core(n):
        return lax.rem(owner(n), 2) == core

    def chunk_of(n):
        h = n // (blocks * per)
        at = pl.multiple_of((n - h * blocks * per) * 128, 128)
        return gathered.at[pl.ds(pl.multiple_of(h * HB, HB), HB), pl.ds(at, 128)]

    def share(k, n):
        return pltpu.make_async_remote_copy(
            src_ref=chunk_of(n),
            dst_ref=chunk_of(n),
            send_sem=send_2.at[k - 1],
            recv_sem=recv_2.at[n],
            device_id=device(lax.rem(me + k, count)),
            device_id_type=MESH,
        )

    row1 = lanes((HB, 128), 0)

    def hand_over(pair):
        for n in range(2 * per):
            chunk = pair * 2 * per + n
            if stride == 1:
                if n % 2 == 0:
                    pass_on(chunk + core).start()
                continue

            @pl.when(jnp.logical_not(same_core(chunk)))
            def _(chunk=chunk):
                pass_on(chunk).start()

    def settle(chunk):
        pass_on(chunk).wait_recv()
        one, two = part_ref[chunk], pair_ref[chunk]
        first, second = one[head + 1 : head + 2], two[head + 1 : head + 2]
        top = jnp.maximum(first, second)
        both = one * jnp.exp2(first - top) + two * jnp.exp2(second - top)
        part_ref[chunk] = jnp.where(row1 == head + 1, top, both)

        @pl.when(owner(chunk) != me)
        def _():
            give(chunk, away(chunk)).start()

    def hand_out(pair):
        for n in range(2 * per):
            chunk = pair * 2 * per + n
            if stride == 1:
                if n % 2 == 0:
                    settle(chunk + 1 - core)
                continue

            @pl.when(same_core(chunk))
            def _(chunk=chunk):
                settle(chunk)

    def finish():
        def arrive(k, carry):
            give(own_chunk, k).wait_recv()
            return carry

        lax.fori_loop(1, chips, arrive, 0)
        piece, others = part_ref[own_chunk], inbox[...]
        level, levels = piece[head + 1 : head + 2], others[:, head + 1 : head + 2]
        top = jnp.maximum(level, jnp.max(levels, axis=0))
        summed = piece * jnp.exp2(level - top) + jnp.sum(others * jnp.exp2(levels - top), axis=0)
        pooled = jnp.where(row1 < head, summed / summed[head : head + 1], 0.0)
        chunk_of(own_chunk)[...] = pooled.astype(BF)

        def share_start(k, carry):
            share(k, own_chunk).start()
            return carry

        lax.fori_loop(1, count, share_start, 0)

    LAG = 4
    own_pair = own_chunk // (2 * per)
    top_a = score(0, sa_ref)

    def attend(pair, top_a):
        index = pair * 2
        top_b = score(index + 1, sb_ref)
        absorb(index, sa_ref, top_a)
        top_a = score(index + 2, sa_ref)
        absorb(index + 1, sb_ref, top_b)
        hand_over(pair)

        @pl.when(pair > 0)
        def _():
            hand_out(pair - 1)

        @pl.when(mine & (own_pair + LAG == pair))
        def _():
            finish()

        return top_a

    pairs = total // 2
    top_a = lax.fori_loop(0, pairs - 1, attend, top_a)
    top_b = score(total - 1, sb_ref)
    absorb(total - 2, sa_ref, top_a)
    absorb(total - 1, sb_ref, top_b)
    hand_over(pairs - 1)
    hand_out(pairs - 2)
    hand_out(pairs - 1)

    @pl.when(mine & (own_pair + LAG >= pairs - 1))
    def _():
        finish()

    def collect(n, carry):
        @pl.when(owner(n) != me)
        def _():
            share(1, n).wait_recv()

        return carry

    lax.fori_loop(0, chunks, collect, 0)
    pooled_ref[...] = jnp.dot(projt_ref[...], gathered[...], preferred_element_type=F32)
    keep.wait()

    def given(n, carry):
        @pl.when(same_core(n) & (owner(n) != me))
        def _():
            give(n, away(n)).wait_send()

        @pl.when(jnp.logical_not(same_core(n)))
        def _():
            pass_on(n).wait_send()

        return carry

    lax.fori_loop(0, chunks, given, 0)

    @pl.when(mine)
    def _():
        def shared(k, carry):
            share(k, own_chunk).wait_send()
            return carry

        lax.fori_loop(1, count, shared, 0)

    for d, (dr, dc) in enumerate(SIDES):

        @pl.when(inside(dr, dc))
        def _(d=d):
            copy(d).wait_send()


def whole_kernel(nr, nc, number, *refs):
    given, outs, held = refs[:number], refs[number : number + 2], refs[number + 2 : 2 * number + 2]
    sems, rest = refs[2 * number + 2], refs[2 * number + 3 :]
    loads = [pltpu.make_async_copy(given[n], held[n], sems.at[n]) for n in range(number)]
    for load in loads:
        load.start()
    block_kernel(nr, nc, loads, *held, *outs, *rest)


def whole(feature, mask, dw_weight, dw_bias, ln_gain, ln_bias, w_in, b_in, w_out, b_out, scale, wk, wv, queries, proj):
    nr, nc = lax.axis_size("row"), lax.axis_size("col")
    rows, channels, cols = feature.shape
    hidden = w_in.shape[1]
    positions = rows * cols
    wide = NH * HB
    number = queries.shape[1]
    qb = 256
    chunks = NH * number // 128
    others, chips = nr * nc - 1, nr * nc // 2
    full = pl.BlockSpec(memory_space=pltpu.VMEM)
    args = (feature, mask, dw_weight, dw_bias, ln_gain, ln_bias, w_in, b_in, w_out, b_out, scale, wk, wv, queries, proj)
    return pl.pallas_call(
        functools.partial(whole_kernel, nr, nc, len(args)),
        out_shape=[
            jax.ShapeDtypeStruct((rows, channels, cols), BF),
            jax.ShapeDtypeStruct((channels, number), F32),
        ],
        in_specs=[pl.BlockSpec(memory_space=pltpu.HBM)] * len(args),
        out_specs=[pl.BlockSpec(memory_space=pltpu.HBM), full],
        scratch_shapes=[pltpu.VMEM(a.shape, a.dtype) for a in args]
        + [
            pltpu.SemaphoreType.DMA((len(args),)),
            pltpu.VMEM((rows, channels, cols), BF),
            pltpu.SemaphoreType.DMA,
            pltpu.VMEM((positions, wide), BF),
            pltpu.VMEM((wide, positions), BF),
            pltpu.VMEM((2, 3, channels, cols), BF),
            pltpu.VMEM((2, channels, 128), BF),
            pltpu.VMEM((2, channels, 128), BF),
            pltpu.VMEM((2, 128, channels), BF),
            pltpu.VMEM((128, channels), BF),
            pltpu.VMEM((3, rows * channels, 128), F32),
            pltpu.VMEM((3, 8 * channels, 128), F32),
            pltpu.VMEM((2, rows * channels, 128), F32),
            pltpu.VMEM((128, 256), F32),
            pltpu.VMEM((256, 128), F32),
            pltpu.VMEM((5, channels, 256), F32),
            pltpu.VMEM((channels, hidden), BF),
            pltpu.VMEM((hidden, channels + 16), BF),
            pltpu.VMEM((2 * wide, channels + 16), BF),
            pltpu.VMEM((NH, wide, number), BF),
            pltpu.VMEM((positions, qb), F32),
            pltpu.VMEM((positions, qb), F32),
            pltpu.VMEM((chunks, HB, 128), F32),
            pltpu.VMEM((chunks, HB, 128), F32),
            pltpu.VMEM((chips - 1, HB, 128), F32),
            pltpu.VMEM((wide, number), BF),
            pltpu.VMEM((channels, wide), BF),
            pltpu.SemaphoreType.DMA((8,)),
            pltpu.SemaphoreType.DMA((8,)),
            pltpu.SemaphoreType.DMA((chunks,)),
            pltpu.SemaphoreType.DMA((chunks,)),
            pltpu.SemaphoreType.DMA((chunks,)),
            pltpu.SemaphoreType.DMA((chips - 1,)),
            pltpu.SemaphoreType.DMA((others,)),
            pltpu.SemaphoreType.DMA((chunks,)),
        ],
        compiler_params=pltpu.CompilerParams(
            collective_id=0, has_side_effects=True, vmem_limit_bytes=60 << 20
        ),
        name="whole",
    )(*args)


def body(
    feature,
    mask,
    dw_weight,
    dw_bias,
    ln_gain,
    ln_bias,
    w_in,
    b_in,
    w_out,
    b_out,
    layer_scale,
    w_key,
    w_value,
    queries,
    w_proj,
):
    block_out, pooled = whole(
        jnp.transpose(feature, (0, 2, 1)),
        mask,
        dw_weight,
        dw_bias,
        ln_gain,
        ln_bias,
        w_in,
        b_in,
        jnp.transpose(w_out),
        b_out,
        layer_scale,
        w_key,
        w_value,
        jnp.transpose(queries),
        w_proj,
    )
    return (jnp.transpose(block_out, (0, 2, 1)), jnp.transpose(pooled))


def solution(mesh):
    return jax.shard_map(
        body,
        mesh=mesh,
        in_specs=(P("row", "col", None), P("row", "col")) + (P(),) * 13,
        out_specs=(P("row", "col", None), P()),
        check_vma=False,
    )
```

```python
import functools
import math

import jax
import jax.numpy as jnp
from jax import lax
from jax.experimental import pallas as pl
from jax.experimental.pallas import tpu as pltpu
from jax.sharding import PartitionSpec as P

NH = 8
HB = 32
LOW = -1e29
MASKED = -1e30
MESH = pl.DeviceIdType.MESH
SIDES = [(0, -1), (0, 1), (-1, 0), (1, 0), (-1, -1), (-1, 1), (1, -1), (1, 1)]
BF, F32 = jnp.bfloat16, jnp.float32


def lanes(shape, axis=1):
    return lax.broadcasted_iota(jnp.int32, shape, axis)


def block_kernel(
    nr,
    nc,
    loads,
    x_ref,
    mask_ref,
    dw_ref,
    dwb_ref,
    gain_ref,
    shift_ref,
    win_ref,
    bin_ref,
    wout_ref,
    bout_ref,
    scale_ref,
    wk_ref,
    wv_ref,
    raw_ref,
    proj_ref,
    out_hbm,
    pooled_ref,
    out_ref,
    out_sem,
    k_ref,
    vt_ref,
    line_ref,
    strip_ref,
    strip_in,
    corner_ref,
    corner_in,
    s_ref,
    z_ref,
    conv_ref,
    tap_ref,
    base_ref,
    col_ref,
    half_ref,
    wint_ref,
    wkv_ref,
    q_ref,
    sa_ref,
    sb_ref,
    part_ref,
    pair_ref,
    inbox,
    gathered,
    projt_ref,
    send,
    recv,
    send_0,
    recv_0,
    send_1,
    recv_1,
    send_2,
    recv_2,
):
    r, c = lax.axis_index("row"), lax.axis_index("col")
    rows, channels, cols = x_ref.shape
    head = channels // NH

    def inside(dr, dc):
        return (r + dr >= 0) & (r + dr < nr) & (c + dc >= 0) & (c + dc < nc)

    me = r * nc + c
    count = nr * nc

    def device(p):
        return (p // nc, lax.rem(p, nc))

    barrier = pltpu.get_barrier_semaphore()

    def greet(k, carry):
        pl.semaphore_signal(
            barrier, inc=1, device_id=device(lax.rem(me + k, count)), device_id_type=MESH
        )
        return carry

    lax.fori_loop(1, count, greet, 0)

    lane = lanes((channels, 128))

    def pack(i, carry):
        low, high = carry
        x = x_ref[i]
        own = (lane >= 8 * i) & (lane < 8 * i + 3)
        low = jnp.where(own, pltpu.roll(x[:, 0:128], 8 * i, 1), low)
        high = jnp.where(own, pltpu.roll(x[:, cols - 128 : cols], 8 * i + 3, 1), high)
        return low, high

    zero = jnp.zeros((channels, 128), F32)
    loads[0].wait()
    edges = lax.fori_loop(0, rows, pack, (zero.astype(BF), zero.astype(BF)))
    for e in range(2):
        strip_ref[e] = edges[e]
        corner_ref[e] = jnp.transpose(edges[e].astype(F32)).astype(BF)

    pl.semaphore_wait(barrier, count - 1)

    def copy(d):
        dr, dc = SIDES[d]
        if dr == 0:
            src = strip_ref.at[0 if dc < 0 else 1]
            dst = strip_in.at[1 if dc < 0 else 0]
        elif dc == 0:
            src = x_ref.at[pl.ds(0 if dr < 0 else rows - 3, 3)]
            dst = line_ref.at[1 if dr < 0 else 0]
        else:
            src = corner_ref.at[0 if dc < 0 else 1, pl.ds(0 if dr < 0 else 96, 32)]
            dst = corner_in.at[pl.ds((64 if dc < 0 else 0) + (32 if dr < 0 else 0), 32)]
        return pltpu.make_async_remote_copy(
            src_ref=src,
            dst_ref=dst,
            send_sem=send.at[d],
            recv_sem=recv.at[d],
            device_id=(r + dr, c + dc),
            device_id_type=MESH,
        )

    for d, (dr, dc) in enumerate(SIDES):

        @pl.when(inside(dr, dc))
        def _(d=d):
            copy(d).start()

        @pl.when(jnp.logical_not(inside(-dr, -dc)))
        def _(d=d, dr=dr, dc=dc):
            if dr == 0:
                strip_in[1 if dc < 0 else 0] = jnp.zeros((channels, 128), BF)
            elif dc == 0:
                line_ref[1 if dr < 0 else 0] = jnp.zeros((3, channels, cols), BF)
            else:
                at = (64 if dc < 0 else 0) + (32 if dr < 0 else 0)
                corner_in[at : at + 32] = jnp.zeros((32, channels), BF)

    for load in loads[1:]:
        load.wait()

    tap_ref[...] = jnp.zeros_like(tap_ref)
    for a in range(7):
        for b in range(7):
            at = (b * 16 + a - 3) % 128
            tap_ref[at : at + 1, 0:channels] = dw_ref[a, b : b + 1, :]
    base_ref[...] = jnp.transpose(tap_ref[...])

    def column(vector, size):
        wide = jnp.broadcast_to(vector[None, :], (128, size))
        return jnp.transpose(wide)

    for n, ref in enumerate((dwb_ref, gain_ref, shift_ref, bout_ref, scale_ref)):
        wide = column(ref[...], channels)
        col_ref[n, :, 0:128] = wide
        col_ref[n, :, 128:256] = wide
    level = jnp.broadcast_to(bin_ref[...][None, :], (8, bin_ref.shape[0]))
    row8 = lanes(level.shape, 0)
    terms = jnp.zeros_like(level)
    for n in range(3):
        term = level.astype(BF).astype(F32)
        terms = jnp.where(row8 == n, term, terms)
        level = level - term
    stack = jnp.concatenate([win_ref[...].astype(F32), terms, jnp.zeros_like(terms)], axis=0)
    wint_ref[...] = jnp.transpose(stack).astype(BF)
    half_ref[...] = (wout_ref[...].astype(F32) * 0.5).astype(BF)
    pad = jnp.zeros((HB - head, channels), F32)
    mark_row, mark_lane = lanes((HB, 16), 0), lanes((HB, 16), 1)
    for n, ref in enumerate((wk_ref, wv_ref)):
        turned = jnp.transpose(ref[...].astype(F32))
        for h in range(NH):
            piece = jnp.concatenate([turned[h * head : (h + 1) * head], pad], axis=0)
            tag = 1.0 if n == 1 else (1.0 if h == 0 else 0.0)
            mark = jnp.where((mark_row == head) & (mark_lane == (0 if n == 1 else 1)), tag, 0.0)
            at = n * NH * HB + h * HB
            wkv_ref[at : at + HB, :] = jnp.concatenate([piece, mark], axis=1).astype(BF)

    turned = []
    proj = proj_ref[...].astype(F32)
    for h in range(NH):
        turned += [proj[h * head : (h + 1) * head], pad]
    projt_ref[...] = jnp.transpose(jnp.concatenate(turned, axis=0)).astype(BF)
    queries = raw_ref.shape[1]
    raw = raw_ref[...].astype(F32)
    one = jnp.where(lanes((HB - head, queries), 0) == 0, 1.0, 0.0)
    for h in range(NH):
        q_ref[h] = jnp.zeros((NH * HB, queries), BF)
        if h > 0:
            q_ref[h, 16:32] = jnp.concatenate([jnp.zeros((8, queries), F32), one], axis=0).astype(BF)
        own = jnp.concatenate([raw[h * head : (h + 1) * head], one if h == 0 else one * 0.0], axis=0)
        q_ref[h, h * HB : (h + 1) * HB] = own.astype(BF)

    def widen(i, carry):
        x = x_ref[i].astype(F32)
        at = pl.multiple_of(i * channels, channels)
        s_ref[0, pl.ds(at, channels)] = x[:, 0:128]
        s_ref[1, pl.ds(at, channels)] = x[:, 128:256]
        return carry

    lax.fori_loop(0, rows, widen, 0)

    def land(d):
        dr, dc = SIDES[d]

        @pl.when(inside(-dr, -dc))
        def _():
            copy(d).wait_recv()

    land(0)
    land(1)

    def side(low, high):
        return jnp.where(lane < 3, low, jnp.where(lane >= 125, high, 0.0))

    def unpack(i, carry):
        left = pltpu.roll(strip_in[0], 125 + (128 - 8 * i), 1).astype(F32)
        right = pltpu.roll(strip_in[1], 128 - 8 * i, 1).astype(F32)
        at = pl.multiple_of(i * channels, channels)
        s_ref[2, pl.ds(at, channels)] = side(right, left)
        return carry

    lax.fori_loop(0, rows, unpack, 0)

    out_row = lanes((rows, 128), 0)
    in_row = lanes((rows, 128), 1) % 16
    near = (in_row - out_row <= 3) & (out_row - in_row <= 3)

    def bands(ch, keep):
        tap = jnp.broadcast_to(base_ref[pl.ds(ch, 1), :], (rows, 128))
        band = jnp.where(keep, pltpu.roll(tap, 0, 1, stride=1, stride_axis=0), 0.0)
        high = band.astype(BF)
        low = (band - high.astype(F32)).astype(BF)
        return jnp.concatenate([high, low], axis=0)

    UN = 96

    def local(step, carry):
        for u in range(UN):
            ch = step * UN + u
            x = jnp.concatenate(
                [s_ref[t, pl.ds(ch, rows, stride=channels), :] for t in range(3)], axis=1
            ).astype(BF)
            parts = [pltpu.roll(x, (3 - b) % 384, 1)[:, 0:cols] for b in range(7)]
            band = bands(ch, near)
            y = jnp.dot(
                band[:, 0:112], jnp.concatenate(parts, axis=0), preferred_element_type=F32
            )
            y = y[0:rows] + y[rows : 2 * rows]
            at = pl.multiple_of(ch * rows, rows)
            conv_ref[0, pl.ds(at, rows)] = y[:, 0:128]
            conv_ref[1, pl.ds(at, rows)] = y[:, 128:256]
        return carry

    lax.fori_loop(0, channels // UN, local, 0)

    row16 = lanes((16, cols), 0)
    ones16 = jnp.where(row16 < 3, 1.0, 0.0).astype(BF)

    def norm(row):
        flat = jnp.concatenate(
            [conv_ref[t, pl.ds(row, channels, stride=rows), :] for t in range(2)], axis=1
        )
        flat = flat + col_ref[0]
        average = jnp.sum(flat, axis=0, keepdims=True) * (1.0 / channels)
        moved = flat - average
        spread = jnp.sum(moved * moved, axis=0, keepdims=True) * (1.0 / channels)
        normed = (moved * lax.rsqrt(spread + 1e-06) * col_ref[1] + col_ref[2]).astype(BF)
        return jnp.concatenate([normed, ones16], axis=0)

    def expand(normed):
        inner = jnp.dot(wint_ref[...], normed, preferred_element_type=F32)
        return (inner * (1.0 + lax.erf(inner * math.sqrt(0.5)))).astype(BF)

    def contract(row, act):
        branch = jnp.dot(half_ref[...], act, preferred_element_type=F32) + col_ref[3]
        result = (x_ref[row].astype(F32) + col_ref[4] * branch).astype(BF)
        out_ref[row] = result
        bias = jnp.where(mask_ref[pl.ds(row, 1), :] > 0, 0.0, MASKED)
        extra = jnp.where(row16 == 0, 1.0, jnp.where(row16 == 1, bias, 0.0)).astype(BF)
        result = jnp.concatenate([result, extra], axis=0)
        both = jnp.dot(wkv_ref[...], result, preferred_element_type=F32)
        keys, values = both[0 : NH * HB], both[NH * HB : 2 * NH * HB]
        at = pl.multiple_of(row * cols, cols)
        k_ref[pl.ds(at, cols), :] = jnp.transpose(keys).astype(BF)
        vt_ref[:, pl.ds(at, cols)] = values.astype(BF)

    def mlp(numbers):
        size = len(numbers)
        normed, act = {}, {}
        for n in range(size + 2):
            if n < size:
                normed[n] = norm(numbers[n])
            if 0 <= n - 1 < size:
                act[n - 1] = expand(normed.pop(n - 1))
            if 0 <= n - 2:
                contract(numbers[n - 2], act.pop(n - 2))

    mlp(list(range(3, rows - 3)))

    for d in range(2, 8):
        land(d)

    turned = jnp.transpose(corner_in[...].astype(F32))
    for s in range(8):
        at = s * channels
        if s < 3:
            line = line_ref[1, s].astype(F32)
            right, left = 96 + 8 * s, 32 + 8 * s
        elif s > 4:
            line = line_ref[0, s - 5].astype(F32)
            right, left = 64 + 8 * (s - 4), 8 * (s - 4)
        else:
            for t in range(3):
                z_ref[t, at : at + channels] = zero
            continue
        z_ref[0, at : at + channels] = line[:, 0:128]
        z_ref[1, at : at + channels] = line[:, 128:256]
        z_ref[2, at : at + channels] = side(
            pltpu.roll(turned, 128 - right, 1), pltpu.roll(turned, (125 - left) % 128, 1)
        )

    far = jnp.logical_not(near)

    def outer(step, carry):
        for u in range(UN):
            ch = step * UN + u
            x = jnp.concatenate(
                [z_ref[t, pl.ds(ch, 8, stride=channels), :] for t in range(3)], axis=1
            )
            parts = [pltpu.roll(x, (3 - b) % 384, 1)[:, 0:cols] for b in range(7)]
            groups = []
            for g in range(8):
                groups += [parts[max(g - 1, 0)], parts[(g + 1) % 8 if g != 6 else 0]]
            band = bands(ch, far)
            y = jnp.dot(
                band, jnp.concatenate(groups, axis=0).astype(BF), preferred_element_type=F32
            )
            y = y[0:rows] + y[rows : 2 * rows]
            at = pl.multiple_of(ch * rows, rows)
            conv_ref[0, pl.ds(at, rows)] += y[:, 0:128]
            conv_ref[1, pl.ds(at, rows)] += y[:, 128:256]
        return carry

    lax.fori_loop(0, channels // UN, outer, 0)

    mlp([0, 1, 2, rows - 3, rows - 2, rows - 1])

    keep = pltpu.make_async_copy(out_ref, out_hbm, out_sem)
    keep.start()

    qb = sa_ref.shape[1]
    blocks = queries // qb
    total = NH * blocks
    factor = math.log2(math.e) / math.sqrt(head)
    per = qb // 128
    chunks = total * per
    stride = count // chunks
    row = lanes((HB, qb), 0)

    def owner(n):
        return lax.rem(n * 3 + 23, chunks) * stride

    mine = lax.rem(me, stride) == 0
    own_chunk = lax.rem((me // stride + 9) * 11, chunks)

    def place(index):
        h = index // blocks
        return h, pl.multiple_of((index - h * blocks) * qb, qb)

    def score(index, s_ref):
        h, at = place(index)
        s = jnp.dot(k_ref[...], q_ref[h, :, pl.ds(at, qb)], preferred_element_type=F32)
        s_ref[...] = s
        return jnp.maximum(jnp.max(s, axis=0, keepdims=True), LOW)

    def absorb(index, s_ref, top):
        h, at = place(index)
        e = jnp.exp2((s_ref[...] - top) * factor).astype(BF)
        v = vt_ref[pl.ds(pl.multiple_of(h * HB, HB), HB), :]
        o = jnp.dot(v, e, preferred_element_type=F32)
        o = jnp.where(row == head + 1, top * factor, o)
        for n in range(per):
            part_ref[index * per + n] = o[:, n * 128 : n * 128 + 128]

    chip, core = me // 2, lax.rem(me, 2)
    chips = count // 2

    def pass_on(n):
        return pltpu.make_async_remote_copy(
            src_ref=part_ref.at[n],
            dst_ref=pair_ref.at[n],
            send_sem=send_0.at[n],
            recv_sem=recv_0.at[n],
            device_id=device(chip * 2 + 1 - core),
            device_id_type=MESH,
        )

    def give(n, k):
        return pltpu.make_async_remote_copy(
            src_ref=part_ref.at[n],
            dst_ref=inbox.at[k - 1],
            send_sem=send_1.at[n],
            recv_sem=recv_1.at[k - 1],
            device_id=device(owner(n)),
            device_id_type=MESH,
        )

    def away(n):
        return lax.rem(owner(n) // 2 - chip + chips, chips)

    def same_core(n):
        return lax.rem(owner(n), 2) == core

    def chunk_of(n):
        h = n // (blocks * per)
        at = pl.multiple_of((n - h * blocks * per) * 128, 128)
        return gathered.at[pl.ds(pl.multiple_of(h * HB, HB), HB), pl.ds(at, 128)]

    def share(k, n):
        return pltpu.make_async_remote_copy(
            src_ref=chunk_of(n),
            dst_ref=chunk_of(n),
            send_sem=send_2.at[k - 1],
            recv_sem=recv_2.at[n],
            device_id=device(lax.rem(me + k, count)),
            device_id_type=MESH,
        )

    row1 = lanes((HB, 128), 0)

    def hand_over(pair):
        for n in range(2 * per):
            chunk = pair * 2 * per + n
            if stride == 1:
                if n % 2 == 0:
                    pass_on(chunk + core).start()
                continue

            @pl.when(jnp.logical_not(same_core(chunk)))
            def _(chunk=chunk):
                pass_on(chunk).start()

    def settle(chunk):
        pass_on(chunk).wait_recv()
        one, two = part_ref[chunk], pair_ref[chunk]
        first, second = one[head + 1 : head + 2], two[head + 1 : head + 2]
        top = jnp.maximum(first, second)
        both = one * jnp.exp2(first - top) + two * jnp.exp2(second - top)
        part_ref[chunk] = jnp.where(row1 == head + 1, top, both)

        @pl.when(owner(chunk) != me)
        def _():
            give(chunk, away(chunk)).start()

    def hand_out(pair):
        for n in range(2 * per):
            chunk = pair * 2 * per + n
            if stride == 1:
                if n % 2 == 0:
                    settle(chunk + 1 - core)
                continue

            @pl.when(same_core(chunk))
            def _(chunk=chunk):
                settle(chunk)

    def finish():
        def arrive(k, carry):
            give(own_chunk, k).wait_recv()
            return carry

        lax.fori_loop(1, chips, arrive, 0)
        piece, others = part_ref[own_chunk], inbox[...]
        level, levels = piece[head + 1 : head + 2], others[:, head + 1 : head + 2]
        top = jnp.maximum(level, jnp.max(levels, axis=0))
        summed = piece * jnp.exp2(level - top) + jnp.sum(others * jnp.exp2(levels - top), axis=0)
        pooled = jnp.where(row1 < head, summed / summed[head : head + 1], 0.0)
        chunk_of(own_chunk)[...] = pooled.astype(BF)

        def share_start(k, carry):
            share(k, own_chunk).start()
            return carry

        lax.fori_loop(1, count, share_start, 0)

    LAG = 4
    own_pair = own_chunk // (2 * per)
    top_a = score(0, sa_ref)

    def attend(pair, top_a):
        index = pair * 2
        top_b = score(index + 1, sb_ref)
        absorb(index, sa_ref, top_a)
        top_a = score(index + 2, sa_ref)
        absorb(index + 1, sb_ref, top_b)
        hand_over(pair)

        @pl.when(pair > 0)
        def _():
            hand_out(pair - 1)

        @pl.when(mine & (own_pair + LAG == pair))
        def _():
            finish()

        return top_a

    pairs = total // 2
    top_a = lax.fori_loop(0, pairs - 1, attend, top_a)
    top_b = score(total - 1, sb_ref)
    absorb(total - 2, sa_ref, top_a)
    absorb(total - 1, sb_ref, top_b)
    hand_over(pairs - 1)
    hand_out(pairs - 2)
    hand_out(pairs - 1)

    @pl.when(mine & (own_pair + LAG >= pairs - 1))
    def _():
        finish()

    def collect(n, carry):
        @pl.when(owner(n) != me)
        def _():
            share(1, n).wait_recv()

        return carry

    lax.fori_loop(0, chunks, collect, 0)
    pooled_ref[...] = jnp.dot(projt_ref[...], gathered[...], preferred_element_type=F32)
    keep.wait()

    def given(n, carry):
        @pl.when(same_core(n) & (owner(n) != me))
        def _():
            give(n, away(n)).wait_send()

        @pl.when(jnp.logical_not(same_core(n)))
        def _():
            pass_on(n).wait_send()

        return carry

    lax.fori_loop(0, chunks, given, 0)

    @pl.when(mine)
    def _():
        def shared(k, carry):
            share(k, own_chunk).wait_send()
            return carry

        lax.fori_loop(1, count, shared, 0)

    for d, (dr, dc) in enumerate(SIDES):

        @pl.when(inside(dr, dc))
        def _(d=d):
            copy(d).wait_send()


def whole_kernel(nr, nc, number, *refs):
    given, outs, held = refs[:number], refs[number : number + 2], refs[number + 2 : 2 * number + 2]
    sems, rest = refs[2 * number + 2], refs[2 * number + 3 :]
    loads = [pltpu.make_async_copy(given[n], held[n], sems.at[n]) for n in range(number)]
    for load in loads:
        load.start()
    block_kernel(nr, nc, loads, *held, *outs, *rest)


def whole(feature, mask, dw_weight, dw_bias, ln_gain, ln_bias, w_in, b_in, w_out, b_out, scale, wk, wv, queries, proj):
    nr, nc = lax.axis_size("row"), lax.axis_size("col")
    rows, channels, cols = feature.shape
    hidden = w_in.shape[1]
    positions = rows * cols
    wide = NH * HB
    number = queries.shape[1]
    qb = 256
    chunks = NH * number // 128
    others, chips = nr * nc - 1, nr * nc // 2
    full = pl.BlockSpec(memory_space=pltpu.VMEM)
    args = (feature, mask, dw_weight, dw_bias, ln_gain, ln_bias, w_in, b_in, w_out, b_out, scale, wk, wv, queries, proj)
    return pl.pallas_call(
        functools.partial(whole_kernel, nr, nc, len(args)),
        out_shape=[
            jax.ShapeDtypeStruct((rows, channels, cols), BF),
            jax.ShapeDtypeStruct((channels, number), F32),
        ],
        in_specs=[pl.BlockSpec(memory_space=pltpu.HBM)] * len(args),
        out_specs=[pl.BlockSpec(memory_space=pltpu.HBM), full],
        scratch_shapes=[pltpu.VMEM(a.shape, a.dtype) for a in args]
        + [
            pltpu.SemaphoreType.DMA((len(args),)),
            pltpu.VMEM((rows, channels, cols), BF),
            pltpu.SemaphoreType.DMA,
            pltpu.VMEM((positions, wide), BF),
            pltpu.VMEM((wide, positions), BF),
            pltpu.VMEM((2, 3, channels, cols), BF),
            pltpu.VMEM((2, channels, 128), BF),
            pltpu.VMEM((2, channels, 128), BF),
            pltpu.VMEM((2, 128, channels), BF),
            pltpu.VMEM((128, channels), BF),
            pltpu.VMEM((3, rows * channels, 128), F32),
            pltpu.VMEM((3, 8 * channels, 128), F32),
            pltpu.VMEM((2, rows * channels, 128), F32),
            pltpu.VMEM((128, 256), F32),
            pltpu.VMEM((256, 128), F32),
            pltpu.VMEM((5, channels, 256), F32),
            pltpu.VMEM((channels, hidden), BF),
            pltpu.VMEM((hidden, channels + 16), BF),
            pltpu.VMEM((2 * wide, channels + 16), BF),
            pltpu.VMEM((NH, wide, number), BF),
            pltpu.VMEM((positions, qb), F32),
            pltpu.VMEM((positions, qb), F32),
            pltpu.VMEM((chunks, HB, 128), F32),
            pltpu.VMEM((chunks, HB, 128), F32),
            pltpu.VMEM((chips - 1, HB, 128), F32),
            pltpu.VMEM((wide, number), BF),
            pltpu.VMEM((channels, wide), BF),
            pltpu.SemaphoreType.DMA((8,)),
            pltpu.SemaphoreType.DMA((8,)),
            pltpu.SemaphoreType.DMA((chunks,)),
            pltpu.SemaphoreType.DMA((chunks,)),
            pltpu.SemaphoreType.DMA((chunks,)),
            pltpu.SemaphoreType.DMA((chips - 1,)),
            pltpu.SemaphoreType.DMA((others,)),
            pltpu.SemaphoreType.DMA((chunks,)),
        ],
        compiler_params=pltpu.CompilerParams(
            collective_id=0, has_side_effects=True, vmem_limit_bytes=60 << 20
        ),
        name="whole",
    )(*args)


def body(
    feature,
    mask,
    dw_weight,
    dw_bias,
    ln_gain,
    ln_bias,
    w_in,
    b_in,
    w_out,
    b_out,
    layer_scale,
    w_key,
    w_value,
    queries,
    w_proj,
):
    block_out, pooled = whole(
        jnp.transpose(feature, (0, 2, 1)),
        mask,
        dw_weight,
        dw_bias,
        ln_gain,
        ln_bias,
        w_in,
        b_in,
        jnp.transpose(w_out),
        b_out,
        layer_scale,
        w_key,
        w_value,
        jnp.transpose(queries),
        w_proj,
    )
    return (jnp.transpose(block_out, (0, 2, 1)), jnp.transpose(pooled))


def solution(mesh):
    return jax.shard_map(
        body,
        mesh=mesh,
        in_specs=(P("row", "col", None), P("row", "col")) + (P(),) * 13,
        out_specs=(P("row", "col", None), P()),
        check_vma=False,
    )
```
